32 devices in a mesh: fsdp: 16 (over z, y, core), tp: 2 (over x).
Axes of the slice: x: 2, y: 2, z: 4, core: 2. Of those that a mesh axis runs over, the one named last changes fastest.
Arguments:
- block_input: bfloat16 [4096, 2048], P(('fsdp', 'tp')), may hold values from -6 to 6
- segments: int32 [16, 256], P('fsdp'), may hold values from 0 to 3, never falling along the last dimension, each value on 1 to 128 neighbouring positions
- cotangent: bfloat16 [4096, 2048], P(('fsdp', 'tp')), may hold values from -6 to 6
- norm_gain: bfloat16 [1, 2, 2048], P(None, None, 'fsdp'), may hold values from 0.5 to 1.5
- norm_shift: bfloat16 [1, 2, 2048], P(None, None, 'fsdp'), may hold values from -1.5 to 1.5
- qkv_weight: bfloat16 [1, 2048, 3, 2048], P(None, 'fsdp', None, 'tp'), may hold values from -0.125 to 0.125
- qkv_bias: bfloat16 [1, 3, 32, 64], P(None, None, 'tp', 'fsdp'), may hold values from -6 to 6
- out_weight: bfloat16 [1, 2048, 2048], P(None, 'tp', 'fsdp'), may hold values from -0.375 to 0.375
- gate_up_weight: bfloat16 [1, 2048, 2, 5632], P(None, 'fsdp', None, 'tp'), may hold values from -0.125 to 0.125
- down_weight: bfloat16 [1, 5632, 2048], P(None, 'tp', 'fsdp'), may hold values from -0.078125 to 0.078125
Outputs:
- block_output: bfloat16 [4096, 2048], P(('fsdp', 'tp'))
- input_grad: bfloat16 [4096, 2048], P(('fsdp', 'tp'))
- norm_gain_grad: float32 [1, 2, 2048], P(None, None, 'fsdp')
- norm_shift_grad: float32 [1, 2, 2048], P(None, None, 'fsdp')
- qkv_weight_grad: float32 [1, 2048, 3, 2048], P(None, 'fsdp', None, 'tp')
- qkv_bias_grad: float32 [1, 3, 32, 64], P(None, None, 'tp', 'fsdp')
- out_weight_grad: float32 [1, 2048, 2048], P(None, 'tp', 'fsdp')
- gate_up_grad: float32 [1, 2048, 2, 5632], P(None, 'fsdp', None, 'tp')
- down_grad: float32 [1, 5632, 2048], P(None, 'tp', 'fsdp')
The draws below stay inside these ranges and needn't reach their ends.
Inputs may be any that keep to these rules, and one draw needn't show every extreme that they name: `segments`: along each sequence segment numbers never fall; each of the 4 documents has 1 to 128 tokens, one exactly 128.
All inputs are finite; a program needn't handle non-finite values.
Results may differ from the reference program's by a relative error of at most 0.019.
The reference program's roundings to bfloat16 on the way count: a program that leaves them out, or rounds other values in their place, can miss the bound.
Values may be sent and summed in bfloat16 or wider, within the bound.
No kernel may reach another device: no remote copies, remote signals or barrier semaphores. Data moves between devices by JAX's collectives and lax.ppermute only.
A program may use at most 256 MiB of HBM per device.

```python
import math
import jax
import jax.numpy as jnp
import numpy as np
from jax import lax

D = 2048
HEADS = 32
HEAD = 64
FF = 5632
ROTARY = 16
LAYERS = 1
SEQ_LEN = 256
SEQS = 1
SEG_COUNT = 4
SEG_MOST = 128
SEQ_ROWS = 16
TOKENS = 4096
N_FSDP = 16


def draw_qkv_bias(key, part):
    base = jnp.clip(0.3 * jax.random.normal(jax.random.fold_in(key, 1), (LAYERS, 3, HEADS, HEAD), jnp.float32), -1.5, 1.5)
    return base.astype(jnp.bfloat16)


def steps_of(own_key, extent, pieces, low, high):
    def one(dim, blocks):
        steps = jax.random.uniform(jax.random.fold_in(jax.random.fold_in(own_key, 6), dim), (blocks,), jnp.float32, low / len(pieces), high / len(pieces))
        return jnp.repeat(jnp.exp(steps), extent[dim] // blocks).reshape((-1,) + (1,) * (len(extent) - dim - 1))

    factor_of = one(*pieces[0])
    for cut in pieces[1:]:
        factor_of = factor_of * one(*cut)
    return factor_of


def split_up(amount, total, limit, slope):
    loads = [(1 << 20) // math.isqrt(standing ** slope) + 1 for standing in range(2, amount + 1)]
    rest, counts = total - limit - (amount - 1), [1] * (amount - 1)
    while rest > 0:
        movable = [i for i in range(amount - 1) if counts[i] < limit]
        mass, budget = sum([loads[i] for i in movable]), rest
        for i in movable:
            addition = min(limit - counts[i], max(1, budget * loads[i] // mass), rest)
            counts[i] = counts[i] + addition
            rest = rest - addition
    return np.array([limit] + counts)


def uneven(stream_key, number_of, total, most, lean):
    if number_of == 2:
        one = jax.random.randint(stream_key, (), max(1, total - most), min(most, total - 1) + 1)
        return jnp.stack([one, total - one])
    tallies = jnp.asarray(split_up(number_of, total, most, lean), jnp.int32)
    pairs = (number_of - 1) // 2
    source_of, receiver = tallies[1:1 + 2 * pairs:2], tallies[2:2 + 2 * pairs:2]
    room = jnp.minimum(source_of - 1, most - receiver)
    passed = jax.random.randint(jax.random.fold_in(stream_key, 1), (pairs,), 0, 1 << 20) % (room + 1)
    tallies = tallies.at[1:1 + 2 * pairs:2].set(source_of - passed).at[2:2 + 2 * pairs:2].set(receiver + passed)
    return tallies[jax.random.permutation(jax.random.fold_in(stream_key, 2), number_of)]


def scatter_about(own_key, shape, spread, bound, pieces=(), kind=jnp.bfloat16):
    values = spread * jax.random.normal(own_key, shape, jnp.float32)
    if pieces:
        values = values * steps_of(own_key, shape, pieces, -0.22, 0.18)
    return jnp.clip(values, -bound, bound).astype(kind)


def setup_inputs(seed: int = 0) -> dict:
    streams_of = jax.random.split(jax.random.key(seed), 11)
    block_input = scatter_about(streams_of[0], (TOKENS, D), 1.0, 6.0, ((0, 32),))
    segments = jax.vmap(lambda own: jnp.searchsorted(jnp.cumsum(uneven(own, SEG_COUNT, SEQ_LEN, SEG_MOST, 1)), jnp.arange(SEQ_LEN), side="right"))(jax.random.split(streams_of[1], SEQ_ROWS)).reshape((SEQ_ROWS, SEQ_LEN)).astype(jnp.int32)
    cotangent = scatter_about(streams_of[2], (TOKENS, D), 1.0, 6.0, ((0, 32),))
    norm_gain = jnp.clip(1.0 + 0.1 * jax.random.normal(streams_of[3], (LAYERS, 2, D), jnp.float32), 0.5, 1.5).astype(jnp.bfloat16)
    norm_shift = scatter_about(streams_of[4], (LAYERS, 2, D), 0.3, 1.5, ((2, 16),))
    qkv_weight = scatter_about(streams_of[5], (LAYERS, D, 3, D), D ** -0.5, 0.125, ((1, 16), (3, 2)))
    qkv_bias = draw_qkv_bias(jax.random.fold_in(streams_of[10], 71), 0)
    out_weight = scatter_about(streams_of[7], (LAYERS, D, D), (D // 8) ** -0.5, 0.375, ((1, 2), (2, 16)))
    gate_up_weight = scatter_about(streams_of[8], (LAYERS, D, 2, FF), D ** -0.5, 0.125, ((1, 16), (3, 2)))
    down_weight = scatter_about(streams_of[9], (LAYERS, FF, D), FF ** -0.5, 0.078125, ((1, 2), (2, 16)))
    return dict(block_input=block_input, segments=segments, cotangent=cotangent, norm_gain=norm_gain, norm_shift=norm_shift, qkv_weight=qkv_weight, qkv_bias=qkv_bias, out_weight=out_weight, gate_up_weight=gate_up_weight, down_weight=down_weight)


EPS = 1e-05
NEG = -1e+30
SCALE = 0.125
ROPE_BASE = 10000.0

def product(form, left, right):
    return jnp.einsum(form, left.astype(jnp.float32), right.astype(jnp.float32))

def times_transposed(left, right):
    return lax.dot_general(left, right, (((1,), (1,)), ((), ())), preferred_element_type=jnp.float32)

def transposed_times(left, right):
    return lax.dot_general(left, right, (((0,), (0,)), ((), ())), preferred_element_type=jnp.float32)

def norm_forward(rows, gain, shift):
    center = rows - lax.optimization_barrier(jnp.mean(rows, axis=1, keepdims=True))
    inv_std = lax.rsqrt(lax.optimization_barrier(jnp.mean(center * center, axis=1, keepdims=True)) + EPS)
    normed = center * inv_std
    return (normed * gain + shift, normed, inv_std)

def norm_backward(grad_out, normed, inv_std, gain):
    scaled = grad_out * gain
    grad_in = inv_std * (scaled - lax.optimization_barrier(jnp.mean(scaled, axis=1, keepdims=True)) - normed * lax.optimization_barrier(jnp.mean(scaled * normed, axis=1, keepdims=True)))
    return (grad_in, lax.optimization_barrier(jnp.sum(grad_out * normed, axis=0)), lax.optimization_barrier(jnp.sum(grad_out, axis=0)))

def rope_tables(length):
    half = ROTARY // 2
    position = jnp.arange(length).astype(jnp.float32)
    inverse = ROPE_BASE ** (-jnp.arange(half).astype(jnp.float32) * 2.0 / ROTARY)
    angles = position[:, None] * inverse[None, :]
    return (jnp.cos(angles)[:, None, :], jnp.sin(angles)[:, None, :])

def rotate(values, cosine, sine):
    half = ROTARY // 2
    first = values[..., :half]
    second = values[..., half:ROTARY]
    return jnp.concatenate([first * cosine - second * sine, second * cosine + first * sine, values[..., ROTARY:]], axis=-1)

def unrotate(grads, cosine, sine):
    half = ROTARY // 2
    first = grads[..., :half]
    second = grads[..., half:ROTARY]
    return jnp.concatenate([first * cosine + second * sine, second * cosine - first * sine, grads[..., ROTARY:]], axis=-1)

def masked_scores(queries, key_rows, allowed):
    scores = product('bqhd,bkhd->bhqk', queries, key_rows) * SCALE
    return jnp.where(allowed, scores, NEG)

def attend(queries, key_rows, value_rows, allowed):
    scores = masked_scores(queries, key_rows, allowed)
    top = lax.optimization_barrier(jnp.max(scores, axis=-1, keepdims=True))
    log_total = top + jnp.log(lax.optimization_barrier(jnp.sum(jnp.exp(scores - top), axis=-1, keepdims=True)))
    probs = jnp.exp(scores - log_total).astype(jnp.bfloat16)
    mixed = product('bhqk,bkhd->bqhd', probs, value_rows).astype(jnp.bfloat16)
    return (mixed, log_total)

def attend_back(queries, key_rows, value_rows, mixed, log_total, grad_mixed, allowed):
    scores = masked_scores(queries, key_rows, allowed)
    probs = jnp.exp(scores - log_total)
    grad_values = product('bhqk,bqhd->bkhd', probs.astype(jnp.bfloat16), grad_mixed)
    grad_probs = product('bqhd,bkhd->bhqk', grad_mixed, value_rows)
    delta = lax.optimization_barrier(jnp.sum(grad_mixed.astype(jnp.float32) * mixed.astype(jnp.float32), axis=-1))
    delta = jnp.transpose(delta, (0, 2, 1))[..., None]
    grad_scores = (probs * (grad_probs - delta) * SCALE).astype(jnp.bfloat16)
    grad_queries = product('bhqk,bkhd->bqhd', grad_scores, key_rows)
    grad_keys = product('bhqk,bqhd->bkhd', grad_scores, queries)
    return (grad_queries, grad_keys, grad_values)

def layer_forward(resid, weights, cosine, sine, allowed):
    gains, shifts, w_qkv, qkv_shift, w_out, w_gate_up, w_down = weights
    gains = gains.astype(jnp.float32)
    shifts = shifts.astype(jnp.float32)
    width = resid.shape[1]
    first_norm, normed_one, inv_one = norm_forward(resid, gains[0], shifts[0])
    attn_in = first_norm.astype(jnp.bfloat16)
    rows_all = attn_in.shape[0]
    seq_count = allowed.shape[0]
    heads_here = qkv_shift.shape[1]
    projected = jnp.dot(attn_in, w_qkv.reshape(width, -1), preferred_element_type=jnp.float32)
    projected = projected.reshape(rows_all, 3, heads_here, HEAD) + qkv_shift.astype(jnp.float32)
    projected = projected.reshape(seq_count, -1, 3, heads_here, HEAD)
    queries = rotate(projected[:, :, 0], cosine, sine).astype(jnp.bfloat16)
    key_rows = rotate(projected[:, :, 1], cosine, sine).astype(jnp.bfloat16)
    value_rows = projected[:, :, 2].astype(jnp.bfloat16)
    mixed, log_total = attend(queries, key_rows, value_rows, allowed)
    mixed_flat = mixed.reshape(rows_all, -1)
    resid_two = resid + jnp.dot(mixed_flat, w_out, preferred_element_type=jnp.float32)
    second_norm, normed_two, inv_two = norm_forward(resid_two, gains[1], shifts[1])
    mlp_in = second_norm.astype(jnp.bfloat16)
    gate_up = jnp.dot(mlp_in, w_gate_up.reshape(width, -1), preferred_element_type=jnp.float32).reshape(rows_all, 2, -1)
    hidden = (jax.nn.silu(gate_up[:, 0]) * gate_up[:, 1]).astype(jnp.bfloat16)
    resid_three = resid_two + jnp.dot(hidden, w_down, preferred_element_type=jnp.float32)
    saved = (normed_one, inv_one, attn_in, queries, key_rows, value_rows, mixed, log_total, normed_two, inv_two, mlp_in, gate_up, hidden)
    return (resid_three, saved)

def layer_backward(grad_three, saved, weights, cosine, sine, allowed):
    gains, shifts, w_qkv, qkv_shift, w_out, w_gate_up, w_down = weights
    gains = gains.astype(jnp.float32)
    normed_one, inv_one, attn_in, queries, key_rows, value_rows, mixed, log_total, normed_two, inv_two, mlp_in, gate_up, hidden = saved
    width = grad_three.shape[1]
    rows_all = attn_in.shape[0]
    heads_here = qkv_shift.shape[1]
    down_cot = grad_three.astype(jnp.bfloat16)
    grad_hidden = times_transposed(down_cot, w_down)
    grad_down = transposed_times(hidden, down_cot)
    gate = gate_up[:, 0]
    upper = gate_up[:, 1]
    sigma = jax.nn.sigmoid(gate)
    grad_gate = grad_hidden * upper * sigma * (1.0 + gate * (1.0 - sigma))
    grad_up = grad_hidden * gate * sigma
    grad_gu = jnp.stack([grad_gate, grad_up], axis=1).astype(jnp.bfloat16).reshape(rows_all, -1)
    grad_gate_up = transposed_times(mlp_in, grad_gu).reshape(w_gate_up.shape)
    grad_mlp_in = times_transposed(grad_gu, w_gate_up.reshape(width, -1))
    grad_norm_two, gain_two, shift_two = norm_backward(grad_mlp_in, normed_two, inv_two, gains[1])
    grad_two = grad_three + grad_norm_two
    attn_cot = grad_two.astype(jnp.bfloat16)
    grad_mixed = times_transposed(attn_cot, w_out).astype(jnp.bfloat16)
    mixed_flat = mixed.reshape(rows_all, -1)
    grad_out = transposed_times(mixed_flat, attn_cot)
    grad_mixed = grad_mixed.reshape(mixed.shape)
    grad_queries, grad_keys, grad_values = attend_back(queries, key_rows, value_rows, mixed, log_total, grad_mixed, allowed)
    grad_queries = unrotate(grad_queries, cosine, sine)
    grad_keys = unrotate(grad_keys, cosine, sine)
    grad_proj = jnp.stack([grad_queries, grad_keys, grad_values], axis=2).reshape(rows_all, 3, heads_here, HEAD)
    grad_qkv_shift = lax.optimization_barrier(jnp.sum(grad_proj, axis=0))
    grad_proj_low = grad_proj.astype(jnp.bfloat16).reshape(rows_all, -1)
    grad_qkv = transposed_times(attn_in, grad_proj_low).reshape(w_qkv.shape)
    grad_attn_in = times_transposed(grad_proj_low, w_qkv.reshape(width, -1))
    grad_norm_one, gain_one, shift_one = norm_backward(grad_attn_in, normed_one, inv_one, gains[0])
    grad_one = grad_two + grad_norm_one
    norm_terms = jnp.stack([gain_one, gain_two, shift_one, shift_two])
    return (grad_one, (norm_terms, grad_qkv, grad_qkv_shift, grad_out, grad_gate_up, grad_down))

def allowed_mask(seg_rows):
    length = seg_rows.shape[1]
    same = seg_rows[:, :, None] == seg_rows[:, None, :]
    causal = jnp.arange(length)[:, None] >= jnp.arange(length)[None, :]
    return (same & causal[None])[:, None]

def reference(block_input, segments, cotangent, norm_gain, norm_shift, qkv_weight, qkv_bias, out_weight, gate_up_weight, down_weight):
    group_rows = SEQS * SEQ_LEN
    inputs = block_input.reshape(N_FSDP, group_rows, D)
    cots = cotangent.reshape(N_FSDP, group_rows, D)
    seg_groups = segments.reshape(N_FSDP, SEQS, SEQ_LEN)
    cosine, sine = rope_tables(SEQ_LEN)
    weights_all = [(norm_gain[layer], norm_shift[layer], qkv_weight[layer], qkv_bias[layer], out_weight[layer], gate_up_weight[layer], down_weight[layer]) for layer in range(LAYERS)]
    start = tuple(((jnp.zeros((4, D), jnp.float32), jnp.zeros((D, 3, D), jnp.float32), jnp.zeros((3, HEADS, HEAD), jnp.float32), jnp.zeros((D, D), jnp.float32), jnp.zeros((D, 2, FF), jnp.float32), jnp.zeros((FF, D), jnp.float32)) for layer in range(LAYERS)))

    def one_group(carry, item):
        rows, cot_rows, seg_rows = item
        allowed = allowed_mask(seg_rows)
        resid = rows.astype(jnp.float32)
        saved_all = []
        for layer in range(LAYERS):
            resid, saved = layer_forward(resid, weights_all[layer], cosine, sine, allowed)
            saved_all.append(saved)
        grad = cot_rows.astype(jnp.float32)
        new_carry = list(carry)
        for layer in reversed(range(LAYERS)):
            grad, terms = layer_backward(grad, saved_all[layer], weights_all[layer], cosine, sine, allowed)
            new_carry[layer] = jax.tree.map(lambda old, add: old + add, carry[layer], terms)
        return (tuple(new_carry), (resid.astype(jnp.bfloat16), grad.astype(jnp.bfloat16)))
    carry, (outputs, grads) = lax.scan(one_group, start, (inputs, cots, seg_groups))
    block_output = outputs.reshape(TOKENS, D)
    input_grad = grads.reshape(TOKENS, D)
    norm_gain_grad = jnp.stack([carry[layer][0][0:2] for layer in range(LAYERS)])
    norm_shift_grad = jnp.stack([carry[layer][0][2:4] for layer in range(LAYERS)])
    qkv_weight_grad = jnp.stack([carry[layer][1] for layer in range(LAYERS)])
    qkv_bias_grad = jnp.stack([carry[layer][2] for layer in range(LAYERS)])
    out_weight_grad = jnp.stack([carry[layer][3] for layer in range(LAYERS)])
    gate_up_grad = jnp.stack([carry[layer][4] for layer in range(LAYERS)])
    down_grad = jnp.stack([carry[layer][5] for layer in range(LAYERS)])
    return (block_output, input_grad, norm_gain_grad, norm_shift_grad, qkv_weight_grad, qkv_bias_grad, out_weight_grad, gate_up_grad, down_grad)
```

```python
import functools

import jax
import jax.numpy as jnp
from jax import lax
from jax.experimental import pallas as pl
from jax.experimental.pallas import tpu as pltpu
from jax.sharding import PartitionSpec as P

HEAD = 64
ROTARY = 16

EPS = 1e-05
NEG = -1e30
SCALE = 0.125
ROPE_BASE = 10000.0

BF16 = jnp.bfloat16
F32 = jnp.float32


def times(left, right):
    return lax.dot_general(left, right, (((1,), (0,)), ((), ())), preferred_element_type=F32)


def times_transposed(left, right):
    return lax.dot_general(left, right, (((1,), (1,)), ((), ())), preferred_element_type=F32)


class Grid:
    def __init__(self, mesh):
        self.count = mesh.shape["fsdp"]
        column = list(mesh.devices[:, 0])
        spots = [tuple(d.coords) for d in column]
        self.cores = 2 if self.count > 1 and spots[0] == spots[1] else 1
        run = 1
        while run < self.count and spots[run][2] == spots[0][2]:
            run += 1
        self.slow = self.count // run
        self.mid = run // self.cores

    def place(self, slow, mid, core):
        return ((slow % self.slow) * self.mid + mid % self.mid) * self.cores + core % self.cores

    def moves(self, slow=0, mid=0, core=0):
        return [
            (self.place(s, m, c), self.place(s + slow, m + mid, c + core))
            for s in range(self.slow)
            for m in range(self.mid)
            for c in range(self.cores)
        ]

    def shift(self, rows, **by):
        return lax.ppermute(rows, "fsdp", self.moves(**by))

    def order(self):
        here = lax.axis_index("fsdp")
        core = here % self.cores
        mid = (here // self.cores) % self.mid
        slow = here // (self.cores * self.mid)
        step = jnp.arange(self.count, dtype=jnp.int32)
        core = (core + step // (self.mid * self.slow)) % self.cores
        mid = (mid + (step // self.slow) % self.mid) % self.mid
        slow = (slow + step % self.slow) % self.slow
        return ((slow * self.mid + mid) * self.cores + core).astype(jnp.int32)


def flip_kernel(order_ref, rows_ref, out_ref):
    out_ref[...] = rows_ref[...].T


def turned(rows, order):
    tokens, width = rows.shape
    count = order.shape[0]
    block = width // count
    if block % 128:
        return rows.T.reshape(count, block, tokens)[order].reshape(width, tokens)
    return pl.pallas_call(
        flip_kernel,
        grid_spec=pltpu.PrefetchScalarGridSpec(
            num_scalar_prefetch=1,
            grid=(count,),
            in_specs=[pl.BlockSpec((tokens, block), lambda j, order: (0, order[j]))],
            out_specs=pl.BlockSpec((block, tokens), lambda j, order: (j, 0)),
        ),
        out_shape=jax.ShapeDtypeStruct((width, tokens), rows.dtype),
    )(order, rows)


def scatter_product(grid, left, right):
    block = left.shape[0] // grid.count
    per_mid = block * grid.slow
    per_core = per_mid * grid.mid
    from_core = []
    for c in range(1, grid.cores):
        out = times(left[c * per_core : (c + 1) * per_core], right).astype(BF16)
        from_core.append(grid.shift(out, core=c))
    from_mid = []
    for m in range(1, grid.mid):
        part = times(left[m * per_mid : (m + 1) * per_mid], right)
        for got in from_core:
            part = part + got[m * per_mid : (m + 1) * per_mid].astype(F32)
        from_mid.append(grid.shift(part.astype(BF16), mid=m))
    total = None
    from_slow = []
    for s in range(grid.slow):
        span = slice(s * block, (s + 1) * block)
        part = times(left[span], right)
        for got in from_core + from_mid:
            part = part + got[span].astype(F32)
        if s == 0:
            total = part
        else:
            from_slow.append(grid.shift(part.astype(BF16), slow=s))
    for got in from_slow:
        total = total + got.astype(F32)
    return total


def other(rows):
    return lax.ppermute(rows, "tp", [(0, 1), (1, 0)])


def pair(rows):
    return jnp.concatenate([rows, other(rows)], axis=0)


def collect(term):
    half = term.shape[0] // 2
    return term[:half] + other(term[half:].astype(BF16)).astype(F32)


def norm_forward(rows, gain, shift):
    center = rows - jnp.mean(rows, axis=1, keepdims=True)
    inv_std = lax.rsqrt(jnp.mean(center * center, axis=1, keepdims=True) + EPS)
    normed = center * inv_std
    return (normed * gain + shift, normed, inv_std)


def norm_backward(grad_out, normed, inv_std, gain):
    scaled = grad_out * gain
    grad_in = inv_std * (
        scaled
        - jnp.mean(scaled, axis=1, keepdims=True)
        - normed * jnp.mean(scaled * normed, axis=1, keepdims=True)
    )
    return (grad_in, jnp.sum(grad_out * normed, axis=0), jnp.sum(grad_out, axis=0))


def rope_tables(position):
    half = ROTARY // 2
    inverse = ROPE_BASE ** (-jnp.arange(half).astype(F32) * 2.0 / ROTARY)
    angles = position.astype(F32)[:, None] * inverse[None, :]
    return (jnp.cos(angles)[:, None, :], jnp.sin(angles)[:, None, :])


def rotate(values, cosine, sine):
    half = ROTARY // 2
    first = values[..., :half]
    second = values[..., half:ROTARY]
    return jnp.concatenate(
        [first * cosine - second * sine, second * cosine + first * sine, values[..., ROTARY:]],
        axis=-1,
    )


def masked_scores(queries, key_rows, allowed):
    scores = jnp.einsum("qhd,khd->hqk", queries, key_rows, preferred_element_type=F32) * SCALE
    return jnp.where(allowed, scores, NEG)


def attend(queries, key_rows, value_rows, allowed):
    scores = masked_scores(queries, key_rows, allowed)
    top = jnp.max(scores, axis=-1, keepdims=True)
    log_total = top + jnp.log(jnp.sum(jnp.exp(scores - top), axis=-1, keepdims=True))
    probs = jnp.exp(scores - log_total).astype(BF16)
    mixed = jnp.einsum("hqk,khd->qhd", probs, value_rows, preferred_element_type=F32).astype(BF16)
    return (mixed, log_total)


def attend_back(queries, key_rows, value_rows, mixed, log_total, grad_mixed, allowed):
    scores = masked_scores(queries, key_rows, allowed)
    probs = jnp.exp(scores - log_total)
    grad_values = jnp.einsum("hqk,qhd->khd", probs.astype(BF16), grad_mixed, preferred_element_type=F32)
    grad_probs = jnp.einsum("qhd,khd->hqk", grad_mixed, value_rows, preferred_element_type=F32)
    delta = jnp.sum(grad_mixed.astype(F32) * mixed.astype(F32), axis=-1)
    delta = jnp.transpose(delta, (1, 0))[..., None]
    grad_scores = (probs * (grad_probs - delta) * SCALE).astype(BF16)
    grad_queries = jnp.einsum("hqk,khd->qhd", grad_scores, key_rows, preferred_element_type=F32)
    grad_keys = jnp.einsum("hqk,qhd->khd", grad_scores, queries, preferred_element_type=F32)
    return (grad_queries, grad_keys, grad_values)


def shards(
    grid,
    block_input,
    segments,
    cotangent,
    norm_gain,
    norm_shift,
    qkv_weight,
    qkv_bias,
    out_weight,
    gate_up_weight,
    down_weight,
):
    count = grid.count
    mine = block_input.shape[0]
    length = segments.shape[1]
    width = block_input.shape[1]
    block = width // count
    wide = qkv_weight.shape[3]
    heads = qkv_bias.shape[2]
    piece = qkv_bias.shape[3]
    turn = lax.axis_index("tp")

    small = jnp.concatenate(
        [norm_gain.reshape(-1), norm_shift.reshape(-1), qkv_bias.reshape(-1)]
    )
    n_small = small.shape[0]
    small_rows = 16 * (-(-n_small // (16 * wide)))
    small = jnp.pad(small, (0, small_rows * wide - n_small)).reshape(small_rows, wide)
    pack = jnp.concatenate(
        [qkv_weight[0, :, 0], qkv_weight[0, :, 1], qkv_weight[0, :, 2], out_weight[0].T, small], axis=0
    )
    packs = lax.all_gather(pack, "fsdp", axis=0)
    gate_up_all = lax.all_gather(jnp.swapaxes(gate_up_weight[0], 0, 1), "fsdp", axis=1, tiled=True)
    w_down = lax.all_gather(down_weight[0], "fsdp", axis=1, tiled=True)

    w_q, w_k, w_v, w_out_t = (
        packs[:, i * block : (i + 1) * block].reshape(width, wide) for i in range(4)
    )
    small_all = packs[:, 4 * block :].reshape(count, -1)
    gains = jnp.swapaxes(small_all[:, : 2 * block].reshape(count, 2, block), 0, 1).reshape(2, width)
    shifts = jnp.swapaxes(small_all[:, 2 * block : 4 * block].reshape(count, 2, block), 0, 1).reshape(2, width)
    bias = small_all[:, 4 * block : 4 * block + 3 * heads * piece].reshape(count, 3, heads, piece)
    bias = jnp.transpose(bias, (1, 2, 0, 3)).reshape(3, heads * HEAD).astype(F32)
    gains = gains.astype(F32)
    shifts = shifts.astype(F32)
    w_gate = gate_up_all[0]
    w_up = gate_up_all[1]

    position = (jnp.arange(length, dtype=jnp.int32) + turn * mine) % length
    cosine, sine = rope_tables(position)
    seg_row = segments[0]
    seg_row = jnp.where(turn == 0, seg_row, jnp.roll(seg_row, mine))
    allowed = (seg_row[:, None] == seg_row[None, :]) & (position[:, None] >= position[None, :])

    order = grid.order()
    down_cot = pair(cotangent)
    down_cot_t = turned(down_cot, order)
    rows_all = pair(block_input).astype(F32)
    resid = block_input.astype(F32)

    first_norm, _, _ = norm_forward(rows_all, gains[0], shifts[0])
    attn_in = first_norm.astype(BF16)
    queries = (times(attn_in, w_q) + bias[0]).reshape(length, heads, HEAD)
    key_rows = (times(attn_in, w_k) + bias[1]).reshape(length, heads, HEAD)
    value_rows = (times(attn_in, w_v) + bias[2]).reshape(length, heads, HEAD)
    queries = rotate(queries, cosine, sine).astype(BF16)
    key_rows = rotate(key_rows, cosine, sine).astype(BF16)
    value_rows = value_rows.astype(BF16)
    mixed, log_total = attend(queries, key_rows, value_rows, allowed)
    mixed_flat = mixed.reshape(length, -1)
    resid_two = resid + collect(times_transposed(mixed_flat, w_out_t))
    second_norm, normed_two, inv_two = norm_forward(resid_two, gains[1], shifts[1])
    mlp_in = pair(second_norm.astype(BF16))
    gate = times(mlp_in, w_gate)
    upper = times(mlp_in, w_up)
    sigma = jax.nn.sigmoid(gate)
    hidden = (gate * sigma * upper).astype(BF16)
    down_grad = scatter_product(grid, down_cot_t, hidden)
    resid_three = resid_two + collect(times(hidden, w_down))
    block_output = resid_three.astype(BF16)

    grad_three = cotangent.astype(F32)
    grad_hidden = times_transposed(down_cot, w_down)
    grad_gate = (grad_hidden * upper * sigma * (1.0 + gate * (1.0 - sigma))).astype(BF16)
    grad_up = (grad_hidden * gate * sigma).astype(BF16)
    mlp_in_t = turned(mlp_in, order)
    gate_grad = scatter_product(grid, mlp_in_t, grad_gate)
    up_grad = scatter_product(grid, mlp_in_t, grad_up)
    grad_mlp_in = collect(times_transposed(grad_gate, w_gate) + times_transposed(grad_up, w_up))
    grad_norm_two, gain_two, shift_two = norm_backward(grad_mlp_in, normed_two, inv_two, gains[1])
    grad_two = grad_three + grad_norm_two
    attn_cot = pair(grad_two.astype(BF16))
    grad_mixed = times(attn_cot, w_out_t).astype(BF16).reshape(mixed.shape)
    out_grad = scatter_product(grid, turned(attn_cot, order), mixed_flat)
    grad_queries, grad_keys, grad_values = attend_back(
        queries, key_rows, value_rows, mixed, log_total, grad_mixed, allowed
    )
    grad_queries = rotate(grad_queries, cosine, -sine)
    grad_keys = rotate(grad_keys, cosine, -sine)
    bias_terms = jnp.stack([jnp.sum(g, axis=0) for g in (grad_queries, grad_keys, grad_values)])
    attn_in_t = turned(attn_in, order)
    grad_proj = [g.astype(BF16).reshape(length, -1) for g in (grad_queries, grad_keys, grad_values)]
    qkv_grad = [scatter_product(grid, attn_in_t, g) for g in grad_proj]
    grad_attn_in = collect(
        times_transposed(grad_proj[0], w_q)
        + times_transposed(grad_proj[1], w_k)
        + times_transposed(grad_proj[2], w_v)
    )
    _, normed_one, inv_one = norm_forward(resid, gains[0], shifts[0])
    grad_norm_one, gain_one, shift_one = norm_backward(grad_attn_in, normed_one, inv_one, gains[0])
    input_grad = (grad_two + grad_norm_one).astype(BF16)

    norm_terms = jnp.stack([gain_one, gain_two, shift_one, shift_two])
    norm_terms = jnp.swapaxes(norm_terms.reshape(4, count, block), 0, 1).reshape(count, 4 * block)
    bias_terms = jnp.transpose(bias_terms.reshape(3, heads, count, piece), (2, 0, 1, 3)).reshape(count, -1)
    terms = jnp.concatenate([norm_terms, bias_terms], axis=1)
    n_terms = terms.shape[1]
    term_rows = 8 * (-(-n_terms // (8 * 128)))
    terms = jnp.pad(terms, ((0, 0), (0, term_rows * 128 - n_terms))).reshape(count * term_rows, 128)
    terms = lax.psum_scatter(terms, "fsdp", scatter_dimension=0, tiled=True).reshape(-1)
    norm_part = terms[: 4 * block].reshape(4, block)
    norm_part = norm_part + other(norm_part)
    bias_part = terms[4 * block : n_terms].reshape(3, heads, piece)
    return (
        block_output,
        input_grad,
        norm_part[None, 0:2],
        norm_part[None, 2:4],
        jnp.stack(qkv_grad, axis=1)[None],
        bias_part[None],
        out_grad.T[None],
        jnp.stack([gate_grad, up_grad], axis=1)[None],
        down_grad.T[None],
    )


def solution(mesh):
    placed = (
        P(("fsdp", "tp"), None),
        P("fsdp", None),
        P(("fsdp", "tp"), None),
        P(None, None, "fsdp"),
        P(None, None, "fsdp"),
        P(None, "fsdp", None, "tp"),
        P(None, None, "tp", "fsdp"),
        P(None, "tp", "fsdp"),
        P(None, "fsdp", None, "tp"),
        P(None, "tp", "fsdp"),
    )
    return jax.shard_map(
        functools.partial(shards, Grid(mesh)),
        mesh=mesh,
        in_specs=placed,
        out_specs=(
            P(("fsdp", "tp"), None),
            P(("fsdp", "tp"), None),
            P(None, None, "fsdp"),
            P(None, None, "fsdp"),
            P(None, "fsdp", None, "tp"),
            P(None, None, "tp", "fsdp"),
            P(None, "tp", "fsdp"),
            P(None, "fsdp", None, "tp"),
            P(None, "tp", "fsdp"),
        ),
        check_vma=False,
    )
```

```python
import jax
import jax.numpy as jnp
from jax import lax
from jax.experimental import pallas as pl
from jax.experimental.pallas import tpu as pltpu
from jax.sharding import PartitionSpec as P


HEAD = 64
ROTARY = 16

EPS = 1e-05
NEG = -1e30
SCALE = 0.125
ROPE_BASE = 10000.0

BF16 = jnp.bfloat16
F32 = jnp.float32


def times(left, right):
    return lax.dot_general(left, right, (((1,), (0,)), ((), ())), preferred_element_type=F32)


def times_transposed(left, right):
    return lax.dot_general(left, right, (((1,), (1,)), ((), ())), preferred_element_type=F32)


class Grid:
    def __init__(self, mesh):
        self.count = mesh.shape["fsdp"]
        column = list(mesh.devices[:, 0])
        spots = [tuple(d.coords) for d in column]
        self.cores = 2 if self.count > 1 and spots[0] == spots[1] else 1
        run = 1
        while run < self.count and spots[run][2] == spots[0][2]:
            run += 1
        self.slow = self.count // run
        self.mid = run // self.cores

    def place(self, slow, mid, core):
        return ((slow % self.slow) * self.mid + mid % self.mid) * self.cores + core % self.cores

    def moves(self, slow=0, mid=0, core=0):
        return [
            (self.place(s, m, c), self.place(s + slow, m + mid, c + core))
            for s in range(self.slow)
            for m in range(self.mid)
            for c in range(self.cores)
        ]

    def shift(self, rows, **by):
        return lax.ppermute(rows, "fsdp", self.moves(**by))

    def order(self):
        here = lax.axis_index("fsdp")
        core = here % self.cores
        mid = (here // self.cores) % self.mid
        slow = here // (self.cores * self.mid)
        step = jnp.arange(self.count, dtype=jnp.int32)
        core = (core + step // (self.mid * self.slow)) % self.cores
        mid = (mid + (step // self.slow) % self.mid) % self.mid
        slow = (slow + step % self.slow) % self.slow
        return ((slow * self.mid + mid) * self.cores + core).astype(jnp.int32)


def flip_kernel(order_ref, rows_ref, out_ref):
    count = order_ref.shape[0]
    block = rows_ref.shape[1] // count

    def move(j, carry):
        start = pl.multiple_of(order_ref[j] * block, block)
        out_ref[pl.ds(pl.multiple_of(j * block, block), block), :] = rows_ref[:, pl.ds(start, block)].T
        return carry

    lax.fori_loop(0, count, move, 0)


def turned(rows, order):
    tokens, width = rows.shape
    count = order.shape[0]
    block = width // count
    if block % 128:
        return rows.T.reshape(count, block, tokens)[order].reshape(width, tokens)
    return pl.pallas_call(
        flip_kernel,
        grid_spec=pltpu.PrefetchScalarGridSpec(
            num_scalar_prefetch=1,
            grid=(1,),
            in_specs=[pl.BlockSpec((tokens, width), lambda i, order: (0, 0))],
            out_specs=pl.BlockSpec((width, tokens), lambda i, order: (0, 0)),
        ),
        out_shape=jax.ShapeDtypeStruct((width, tokens), rows.dtype),
    )(order, rows)


def scatter_product(grid, left, right):
    block = left.shape[0] // grid.count
    per_mid = block * grid.slow
    per_core = per_mid * grid.mid
    from_core = []
    for c in range(1, grid.cores):
        out = times(left[c * per_core : (c + 1) * per_core], right).astype(BF16)
        from_core.append(grid.shift(out, core=c))
    from_mid = []
    for m in range(1, grid.mid):
        part = times(left[m * per_mid : (m + 1) * per_mid], right)
        for got in from_core:
            part = part + got[m * per_mid : (m + 1) * per_mid].astype(F32)
        part = part.astype(BF16)
        from_mid.append(grid.shift(part, mid=m))
    from_slow = []
    for s in range(grid.slow):
        span = slice(s * block, (s + 1) * block)
        part = times(left[span], right)
        for got in from_core + from_mid:
            part = part + got[span].astype(F32)
        if s == 0:
            total = part
            continue
        part = part.astype(BF16)
        from_slow.append(grid.shift(part, slow=s))
    for got in from_slow:
        total = total + got.astype(F32)
    return total


def other(rows):
    return lax.ppermute(rows, "tp", [(0, 1), (1, 0)])


def pair(rows):
    return jnp.concatenate([rows, other(rows)], axis=0)


def collect(term):
    half = term.shape[0] // 2
    return term[:half] + other(term[half:].astype(BF16)).astype(F32)


def norm_forward(rows, gain, shift):
    center = rows - jnp.mean(rows, axis=1, keepdims=True)
    inv_std = lax.rsqrt(jnp.mean(center * center, axis=1, keepdims=True) + EPS)
    normed = center * inv_std
    return (normed * gain + shift, normed, inv_std)


def norm_backward(grad_out, normed, inv_std, gain):
    scaled = grad_out * gain
    grad_in = inv_std * (
        scaled
        - jnp.mean(scaled, axis=1, keepdims=True)
        - normed * jnp.mean(scaled * normed, axis=1, keepdims=True)
    )
    return (grad_in, jnp.sum(grad_out * normed, axis=0), jnp.sum(grad_out, axis=0))


def rope_tables(position):
    half = ROTARY // 2
    inverse = ROPE_BASE ** (-jnp.arange(half).astype(F32) * 2.0 / ROTARY)
    angles = position.astype(F32)[:, None] * inverse[None, :]
    return (jnp.cos(angles)[:, None, :], jnp.sin(angles)[:, None, :])


def rotate(values, cosine, sine):
    half = ROTARY // 2
    first = values[..., :half]
    second = values[..., half:ROTARY]
    return jnp.concatenate(
        [first * cosine - second * sine, second * cosine + first * sine, values[..., ROTARY:]],
        axis=-1,
    )


def masked_scores(queries, key_rows, allowed):
    scores = jnp.einsum("qhd,khd->hqk", queries, key_rows, preferred_element_type=F32) * SCALE
    return jnp.where(allowed, scores, NEG)


def attend(queries, key_rows, value_rows, allowed):
    scores = masked_scores(queries, key_rows, allowed)
    top = jnp.max(scores, axis=-1, keepdims=True)
    log_total = top + jnp.log(jnp.sum(jnp.exp(scores - top), axis=-1, keepdims=True))
    probs = jnp.exp(scores - log_total).astype(BF16)
    mixed = jnp.einsum("hqk,khd->qhd", probs, value_rows, preferred_element_type=F32).astype(BF16)
    return (mixed, log_total)


def attend_back(queries, key_rows, value_rows, mixed, log_total, grad_mixed, allowed):
    scores = masked_scores(queries, key_rows, allowed)
    probs = jnp.exp(scores - log_total)
    grad_values = jnp.einsum("hqk,qhd->khd", probs.astype(BF16), grad_mixed, preferred_element_type=F32)
    grad_probs = jnp.einsum("qhd,khd->hqk", grad_mixed, value_rows, preferred_element_type=F32)
    delta = jnp.sum(grad_mixed.astype(F32) * mixed.astype(F32), axis=-1)
    delta = jnp.transpose(delta, (1, 0))[..., None]
    grad_scores = (probs * (grad_probs - delta) * SCALE).astype(BF16)
    grad_queries = jnp.einsum("hqk,khd->qhd", grad_scores, key_rows, preferred_element_type=F32)
    grad_keys = jnp.einsum("hqk,qhd->khd", grad_scores, queries, preferred_element_type=F32)
    return (grad_queries, grad_keys, grad_values)


def shards(
    grid,
    block_input,
    segments,
    cotangent,
    norm_gain,
    norm_shift,
    qkv_weight,
    qkv_bias,
    out_weight,
    gate_up_weight,
    down_weight,
):
    count = grid.count
    mine = block_input.shape[0]
    length = segments.shape[1]
    width = block_input.shape[1]
    block = width // count
    wide = qkv_weight.shape[3]
    heads = qkv_bias.shape[2]
    piece = qkv_bias.shape[3]
    turn = lax.axis_index("tp")

    small = jnp.concatenate(
        [norm_gain.reshape(-1), norm_shift.reshape(-1), qkv_bias.reshape(-1)]
    )
    n_small = small.shape[0]
    small_rows = 16 * (-(-n_small // (16 * wide)))
    small = jnp.pad(small, (0, small_rows * wide - n_small)).reshape(small_rows, wide)
    pack = jnp.concatenate(
        [qkv_weight[0, :, 0], qkv_weight[0, :, 1], qkv_weight[0, :, 2], out_weight[0].T, small], axis=0
    )
    packs = lax.all_gather(pack, "fsdp", axis=0)
    gate_up_all = lax.all_gather(jnp.swapaxes(gate_up_weight[0], 0, 1), "fsdp", axis=1, tiled=True)
    w_down = lax.all_gather(down_weight[0], "fsdp", axis=1, tiled=True)

    w_q, w_k, w_v, w_out_t = (
        packs[:, i * block : (i + 1) * block].reshape(width, wide) for i in range(4)
    )
    small_all = packs[:, 4 * block :].reshape(count, -1)
    gains = jnp.swapaxes(small_all[:, : 2 * block].reshape(count, 2, block), 0, 1).reshape(2, width)
    shifts = jnp.swapaxes(small_all[:, 2 * block : 4 * block].reshape(count, 2, block), 0, 1).reshape(2, width)
    bias = small_all[:, 4 * block : 4 * block + 3 * heads * piece].reshape(count, 3, heads, piece)
    bias = jnp.transpose(bias, (1, 2, 0, 3)).reshape(3, heads * HEAD).astype(F32)
    gains = gains.astype(F32)
    shifts = shifts.astype(F32)
    w_gate = gate_up_all[0]
    w_up = gate_up_all[1]

    position = (jnp.arange(length, dtype=jnp.int32) + turn * mine) % length
    cosine, sine = rope_tables(position)
    seg_row = segments[0]
    seg_row = jnp.where(turn == 0, seg_row, jnp.roll(seg_row, mine))
    allowed = (seg_row[:, None] == seg_row[None, :]) & (position[:, None] >= position[None, :])

    order = grid.order()
    down_cot = pair(cotangent)
    down_cot_t = turned(down_cot, order)
    rows_all = pair(block_input).astype(F32)
    resid = block_input.astype(F32)

    first_norm, _, _ = norm_forward(rows_all, gains[0], shifts[0])
    attn_in = first_norm.astype(BF16)
    queries = (times(attn_in, w_q) + bias[0]).reshape(length, heads, HEAD)
    key_rows = (times(attn_in, w_k) + bias[1]).reshape(length, heads, HEAD)
    value_rows = (times(attn_in, w_v) + bias[2]).reshape(length, heads, HEAD)
    queries = rotate(queries, cosine, sine).astype(BF16)
    key_rows = rotate(key_rows, cosine, sine).astype(BF16)
    value_rows = value_rows.astype(BF16)
    mixed, log_total = attend(queries, key_rows, value_rows, allowed)
    mixed_flat = mixed.reshape(length, -1)
    resid_two = resid + collect(times_transposed(mixed_flat, w_out_t))
    second_norm, normed_two, inv_two = norm_forward(resid_two, gains[1], shifts[1])
    mlp_in = pair(second_norm.astype(BF16))
    gate = times(mlp_in, w_gate)
    upper = times(mlp_in, w_up)
    sigma = jax.nn.sigmoid(gate)
    hidden = (gate * sigma * upper).astype(BF16)
    gate, upper, hidden = lax.optimization_barrier((gate, upper, hidden))
    sigma = jax.nn.sigmoid(gate)
    down_grad = scatter_product(grid, down_cot_t, hidden)
    resid_three = resid_two + collect(times(hidden, w_down))
    block_output = resid_three.astype(BF16)

    grad_three = cotangent.astype(F32)
    grad_hidden = times_transposed(down_cot, w_down)
    grad_gate = (grad_hidden * upper * sigma * (1.0 + gate * (1.0 - sigma))).astype(BF16)
    grad_up = (grad_hidden * gate * sigma).astype(BF16)
    mlp_in_t = turned(mlp_in, order)
    half = grad_gate.shape[1] // 2
    gate_grad, up_grad = (
        jnp.concatenate(
            [scatter_product(grid, mlp_in_t, grad[:, :half]), scatter_product(grid, mlp_in_t, grad[:, half:])],
            axis=1,
        )
        for grad in (grad_gate, grad_up)
    )
    grad_mlp_in = collect(times_transposed(grad_gate, w_gate) + times_transposed(grad_up, w_up))
    grad_norm_two, gain_two, shift_two = norm_backward(grad_mlp_in, normed_two, inv_two, gains[1])
    grad_two = grad_three + grad_norm_two
    attn_cot = pair(grad_two.astype(BF16))
    grad_mixed = times(attn_cot, w_out_t).astype(BF16).reshape(mixed.shape)
    out_grad = scatter_product(grid, turned(attn_cot, order), mixed_flat)
    grad_queries, grad_keys, grad_values = attend_back(
        queries, key_rows, value_rows, mixed, log_total, grad_mixed, allowed
    )
    grad_queries = rotate(grad_queries, cosine, -sine)
    grad_keys = rotate(grad_keys, cosine, -sine)
    bias_terms = jnp.stack([jnp.sum(g, axis=0) for g in (grad_queries, grad_keys, grad_values)])
    attn_in_t = turned(attn_in, order)
    grad_proj = [g.astype(BF16).reshape(length, -1) for g in (grad_queries, grad_keys, grad_values)]
    v_grad = scatter_product(grid, attn_in_t, grad_proj[2])
    q_grad = scatter_product(grid, attn_in_t, grad_proj[0])
    k_grad = scatter_product(grid, attn_in_t, grad_proj[1])
    grad_attn_in = collect(
        times_transposed(grad_proj[0], w_q) + times_transposed(grad_proj[1], w_k) + times_transposed(grad_proj[2], w_v)
    )
    _, normed_one, inv_one = norm_forward(resid, gains[0], shifts[0])
    grad_norm_one, gain_one, shift_one = norm_backward(grad_attn_in, normed_one, inv_one, gains[0])
    input_grad = (grad_two + grad_norm_one).astype(BF16)

    norm_terms = jnp.stack([gain_one, gain_two, shift_one, shift_two])
    norm_terms = jnp.swapaxes(norm_terms.reshape(4, count, block), 0, 1).reshape(count, 4 * block)
    bias_terms = jnp.transpose(bias_terms.reshape(3, heads, count, piece), (2, 0, 1, 3)).reshape(count, -1)
    terms = jnp.concatenate([norm_terms, bias_terms], axis=1)
    n_terms = terms.shape[1]
    term_rows = 8 * (-(-n_terms // (8 * 128)))
    terms = jnp.pad(terms, ((0, 0), (0, term_rows * 128 - n_terms))).reshape(count * term_rows, 128)
    terms = lax.psum(terms, "fsdp")
    terms = lax.dynamic_slice_in_dim(terms, lax.axis_index("fsdp") * term_rows, term_rows, 0).reshape(-1)
    norm_part = terms[: 4 * block].reshape(4, block)
    norm_part = norm_part + other(norm_part)
    bias_part = terms[4 * block : n_terms].reshape(3, heads, piece)
    return (
        block_output,
        input_grad,
        norm_part[None, 0:2],
        norm_part[None, 2:4],
        jnp.stack([q_grad, k_grad, v_grad], axis=1)[None],
        bias_part[None],
        out_grad.T[None],
        jnp.stack([gate_grad, up_grad], axis=1)[None],
        down_grad.T[None],
    )


def solution(mesh):
    placed = (
        P(("fsdp", "tp"), None),
        P("fsdp", None),
        P(("fsdp", "tp"), None),
        P(None, None, "fsdp"),
        P(None, None, "fsdp"),
        P(None, "fsdp", None, "tp"),
        P(None, None, "tp", "fsdp"),
        P(None, "tp", "fsdp"),
        P(None, "fsdp", None, "tp"),
        P(None, "tp", "fsdp"),
    )

    def body(*args):
        return shards(Grid(mesh), *args)

    return jax.shard_map(
        body,
        mesh=mesh,
        in_specs=placed,
        out_specs=(
            P(("fsdp", "tp"), None),
            P(("fsdp", "tp"), None),
            P(None, None, "fsdp"),
            P(None, None, "fsdp"),
            P(None, "fsdp", None, "tp"),
            P(None, None, "tp", "fsdp"),
            P(None, "tp", "fsdp"),
            P(None, "fsdp", None, "tp"),
            P(None, "tp", "fsdp"),
        ),
        check_vma=False,
    )
```

```python
import jax
import jax.numpy as jnp
from jax import lax
from jax.experimental import pallas as pl
from jax.experimental.pallas import tpu as pltpu
from jax.sharding import PartitionSpec as P


HEAD = 64
ROTARY = 16

EPS = 1e-05
NEG = -1e30
SCALE = 0.125
ROPE_BASE = 10000.0

BF16 = jnp.bfloat16
F32 = jnp.float32


def times(left, right):
    return lax.dot_general(left, right, (((1,), (0,)), ((), ())), preferred_element_type=F32)


def times_transposed(left, right):
    return lax.dot_general(left, right, (((1,), (1,)), ((), ())), preferred_element_type=F32)


class Grid:
    def __init__(self, mesh):
        self.count = mesh.shape["fsdp"]
        column = list(mesh.devices[:, 0])
        spots = [tuple(d.coords) for d in column]
        self.cores = 2 if self.count > 1 and spots[0] == spots[1] else 1
        run = 1
        while run < self.count and spots[run][2] == spots[0][2]:
            run += 1
        self.slow = self.count // run
        self.mid = run // self.cores

    def place(self, slow, mid, core):
        return ((slow % self.slow) * self.mid + mid % self.mid) * self.cores + core % self.cores

    def moves(self, slow=0, mid=0, core=0):
        return [
            (self.place(s, m, c), self.place(s + slow, m + mid, c + core))
            for s in range(self.slow)
            for m in range(self.mid)
            for c in range(self.cores)
        ]

    def shift(self, rows, **by):
        return lax.ppermute(rows, "fsdp", self.moves(**by))

    def across(self, slow, step):
        return slow ^ step if self.slow == 4 else (slow + step) % self.slow

    def cross(self, rows, step, ends=True, inner=True):
        moves = []
        for s in range(self.slow):
            if ends if s in (0, self.slow - 1) else inner:
                moves += [
                    (self.place(s, m, c), self.place(self.across(s, step), m, c))
                    for m in range(self.mid)
                    for c in range(self.cores)
                ]
        return lax.ppermute(rows, "fsdp", moves)

    def order(self):
        here = lax.axis_index("fsdp")
        core = here % self.cores
        mid = (here // self.cores) % self.mid
        slow = here // (self.cores * self.mid)
        step = jnp.arange(self.count, dtype=jnp.int32)
        core = (core + step // (self.mid * self.slow)) % self.cores
        mid = (mid + (step // self.slow) % self.mid) % self.mid
        slow = self.across(slow, step % self.slow)
        return ((slow * self.mid + mid) * self.cores + core).astype(jnp.int32)


def flip_kernel(order_ref, rows_ref, out_ref):
    count = order_ref.shape[0]
    block = rows_ref.shape[1] // count

    def move(j, carry):
        start = pl.multiple_of(order_ref[j] * block, block)
        out_ref[pl.ds(pl.multiple_of(j * block, block), block), :] = rows_ref[:, pl.ds(start, block)].T
        return carry

    lax.fori_loop(0, count, move, 0)


def turned(rows, order):
    tokens, width = rows.shape
    count = order.shape[0]
    block = width // count
    if block % 128:
        return rows.T.reshape(count, block, tokens)[order].reshape(width, tokens)
    return pl.pallas_call(
        flip_kernel,
        grid_spec=pltpu.PrefetchScalarGridSpec(
            num_scalar_prefetch=1,
            grid=(1,),
            in_specs=[pl.BlockSpec((tokens, width), lambda i, order: (0, 0))],
            out_specs=pl.BlockSpec((width, tokens), lambda i, order: (0, 0)),
        ),
        out_shape=jax.ShapeDtypeStruct((width, tokens), rows.dtype),
    )(order, rows)


def scatter_product(grid, left, right, relay=False):
    block = left.shape[0] // grid.count
    per_mid = block * grid.slow
    per_core = per_mid * grid.mid
    from_core = []
    for c in range(1, grid.cores):
        out = times(left[c * per_core : (c + 1) * per_core], right).astype(BF16)
        from_core.append(grid.shift(out, core=c))
    from_mid = []
    for m in range(1, grid.mid):
        part = times(left[m * per_mid : (m + 1) * per_mid], right)
        for got in from_core:
            part = part + got[m * per_mid : (m + 1) * per_mid].astype(F32)
        part = part.astype(BF16)
        from_mid.append(grid.shift(part, mid=m))

    def part_of(span):
        part = times(left[span], right)
        for got in from_core + from_mid:
            part = part + got[span].astype(F32)
        return part

    total = part_of(slice(0, block))
    from_slow = []
    if relay and grid.slow == 4:
        mine = part_of(slice(block, 4 * block)).astype(BF16)
        got = grid.cross(mine, 1, inner=False)
        near, far, over = (slice(i * block, (i + 1) * block) for i in range(3))
        from_slow.append(got[near])
        sums = {
            1: mine[near],
            2: (mine[far].astype(F32) + got[over].astype(F32)).astype(BF16),
            3: (mine[over].astype(F32) + got[far].astype(F32)).astype(BF16),
        }
        from_slow += [grid.cross(rows, s, ends=False) for s, rows in sums.items()]
    else:
        for s in range(1, grid.slow):
            part = part_of(slice(s * block, (s + 1) * block)).astype(BF16)
            from_slow.append(grid.cross(part, s))
    for got in from_slow:
        total = total + got.astype(F32)
    return total


def other(rows):
    return lax.ppermute(rows, "tp", [(0, 1), (1, 0)])


def pair(rows):
    return jnp.concatenate([rows, other(rows)], axis=0)


def collect(term):
    half = term.shape[0] // 2
    return term[:half] + other(term[half:].astype(BF16)).astype(F32)


def norm_forward(rows, gain, shift):
    center = rows - jnp.mean(rows, axis=1, keepdims=True)
    inv_std = lax.rsqrt(jnp.mean(center * center, axis=1, keepdims=True) + EPS)
    normed = center * inv_std
    return (normed * gain + shift, normed, inv_std)


def norm_backward(grad_out, normed, inv_std, gain):
    scaled = grad_out * gain
    grad_in = inv_std * (
        scaled
        - jnp.mean(scaled, axis=1, keepdims=True)
        - normed * jnp.mean(scaled * normed, axis=1, keepdims=True)
    )
    return (grad_in, jnp.sum(grad_out * normed, axis=0), jnp.sum(grad_out, axis=0))


def rope_tables(position):
    half = ROTARY // 2
    inverse = ROPE_BASE ** (-jnp.arange(half).astype(F32) * 2.0 / ROTARY)
    angles = position.astype(F32)[:, None] * inverse[None, :]
    return (jnp.cos(angles)[:, None, :], jnp.sin(angles)[:, None, :])


def rotate(values, cosine, sine):
    half = ROTARY // 2
    first = values[..., :half]
    second = values[..., half:ROTARY]
    return jnp.concatenate(
        [first * cosine - second * sine, second * cosine + first * sine, values[..., ROTARY:]],
        axis=-1,
    )


def masked_scores(queries, key_rows, allowed):
    scores = jnp.einsum("qhd,khd->hqk", queries, key_rows, preferred_element_type=F32) * SCALE
    return jnp.where(allowed, scores, NEG)


def attend(queries, key_rows, value_rows, allowed):
    scores = masked_scores(queries, key_rows, allowed)
    top = jnp.max(scores, axis=-1, keepdims=True)
    log_total = top + jnp.log(jnp.sum(jnp.exp(scores - top), axis=-1, keepdims=True))
    probs = jnp.exp(scores - log_total).astype(BF16)
    mixed = jnp.einsum("hqk,khd->qhd", probs, value_rows, preferred_element_type=F32).astype(BF16)
    return (mixed, log_total)


def attend_back(queries, key_rows, value_rows, mixed, log_total, grad_mixed, allowed):
    scores = masked_scores(queries, key_rows, allowed)
    probs = jnp.exp(scores - log_total)
    grad_values = jnp.einsum("hqk,qhd->khd", probs.astype(BF16), grad_mixed, preferred_element_type=F32)
    grad_probs = jnp.einsum("qhd,khd->hqk", grad_mixed, value_rows, preferred_element_type=F32)
    delta = jnp.sum(grad_mixed.astype(F32) * mixed.astype(F32), axis=-1)
    delta = jnp.transpose(delta, (1, 0))[..., None]
    grad_scores = (probs * (grad_probs - delta) * SCALE).astype(BF16)
    grad_queries = jnp.einsum("hqk,khd->qhd", grad_scores, key_rows, preferred_element_type=F32)
    grad_keys = jnp.einsum("hqk,qhd->khd", grad_scores, queries, preferred_element_type=F32)
    return (grad_queries, grad_keys, grad_values)


def shards(
    grid,
    block_input,
    segments,
    cotangent,
    norm_gain,
    norm_shift,
    qkv_weight,
    qkv_bias,
    out_weight,
    gate_up_weight,
    down_weight,
):
    count = grid.count
    mine = block_input.shape[0]
    length = segments.shape[1]
    width = block_input.shape[1]
    block = width // count
    wide = qkv_weight.shape[3]
    heads = qkv_bias.shape[2]
    piece = qkv_bias.shape[3]
    turn = lax.axis_index("tp")

    small = jnp.concatenate(
        [norm_gain.reshape(-1), norm_shift.reshape(-1), qkv_bias.reshape(-1)]
    )
    n_small = small.shape[0]
    small_rows = 16 * (-(-n_small // (16 * wide)))
    small = jnp.pad(small, (0, small_rows * wide - n_small)).reshape(small_rows, wide)
    pack = jnp.concatenate(
        [qkv_weight[0, :, 0], qkv_weight[0, :, 1], qkv_weight[0, :, 2], out_weight[0].T, small], axis=0
    )
    packs = lax.all_gather(pack, "fsdp", axis=0)
    gate_up_all = lax.all_gather(jnp.swapaxes(gate_up_weight[0], 0, 1), "fsdp", axis=1, tiled=True)
    w_down = lax.all_gather(down_weight[0], "fsdp", axis=1, tiled=True)

    w_q, w_k, w_v, w_out_t = (
        packs[:, i * block : (i + 1) * block].reshape(width, wide) for i in range(4)
    )
    small_all = packs[:, 4 * block :].reshape(count, -1)
    gains = jnp.swapaxes(small_all[:, : 2 * block].reshape(count, 2, block), 0, 1).reshape(2, width)
    shifts = jnp.swapaxes(small_all[:, 2 * block : 4 * block].reshape(count, 2, block), 0, 1).reshape(2, width)
    bias = small_all[:, 4 * block : 4 * block + 3 * heads * piece].reshape(count, 3, heads, piece)
    bias = jnp.transpose(bias, (1, 2, 0, 3)).reshape(3, heads * HEAD).astype(F32)
    gains = gains.astype(F32)
    shifts = shifts.astype(F32)
    w_gate = gate_up_all[0]
    w_up = gate_up_all[1]

    position = (jnp.arange(length, dtype=jnp.int32) + turn * mine) % length
    cosine, sine = rope_tables(position)
    seg_row = segments[0]
    seg_row = jnp.where(turn == 0, seg_row, jnp.roll(seg_row, mine))
    allowed = (seg_row[:, None] == seg_row[None, :]) & (position[:, None] >= position[None, :])

    order = grid.order()
    down_cot = pair(cotangent)
    down_cot_t = turned(down_cot, order)
    rows_all = pair(block_input).astype(F32)
    resid = block_input.astype(F32)

    first_norm, _, _ = norm_forward(rows_all, gains[0], shifts[0])
    attn_in = first_norm.astype(BF16)
    queries = (times(attn_in, w_q) + bias[0]).reshape(length, heads, HEAD)
    key_rows = (times(attn_in, w_k) + bias[1]).reshape(length, heads, HEAD)
    value_rows = (times(attn_in, w_v) + bias[2]).reshape(length, heads, HEAD)
    queries = rotate(queries, cosine, sine).astype(BF16)
    key_rows = rotate(key_rows, cosine, sine).astype(BF16)
    value_rows = value_rows.astype(BF16)
    mixed, log_total = attend(queries, key_rows, value_rows, allowed)
    mixed_flat = mixed.reshape(length, -1)
    resid_two = resid + collect(times_transposed(mixed_flat, w_out_t))
    second_norm, normed_two, inv_two = norm_forward(resid_two, gains[1], shifts[1])
    mlp_in = pair(second_norm.astype(BF16))
    gate = times(mlp_in, w_gate)
    upper = times(mlp_in, w_up)
    sigma = jax.nn.sigmoid(gate)
    hidden = (gate * sigma * upper).astype(BF16)
    gate, upper, hidden = lax.optimization_barrier((gate, upper, hidden))
    sigma = jax.nn.sigmoid(gate)
    down_grad = scatter_product(grid, down_cot_t, hidden, relay=True)

    grad_three = cotangent.astype(F32)
    grad_hidden = times_transposed(down_cot, w_down)
    grad_gate = (grad_hidden * upper * sigma * (1.0 + gate * (1.0 - sigma))).astype(BF16)
    grad_up = (grad_hidden * gate * sigma).astype(BF16)
    mlp_in_t = turned(mlp_in, order)
    half = grad_gate.shape[1] // 2
    gate_grad, up_grad = (
        jnp.concatenate(
            [
                scatter_product(grid, mlp_in_t, grad[:, :half], relay=True),
                scatter_product(grid, mlp_in_t, grad[:, half:], relay=True),
            ],
            axis=1,
        )
        for grad in (grad_gate, grad_up)
    )
    grad_mlp_in = collect(times_transposed(grad_gate, w_gate) + times_transposed(grad_up, w_up))
    grad_norm_two, gain_two, shift_two = norm_backward(grad_mlp_in, normed_two, inv_two, gains[1])
    grad_two = grad_three + grad_norm_two
    attn_cot = pair(grad_two.astype(BF16))
    attn_cot, hidden_late = lax.optimization_barrier((attn_cot, hidden))
    resid_three = resid_two + collect(times(hidden_late, w_down))
    block_output = resid_three.astype(BF16)
    grad_mixed = times(attn_cot, w_out_t).astype(BF16).reshape(mixed.shape)
    out_grad = scatter_product(grid, turned(attn_cot, order), mixed_flat)
    grad_queries, grad_keys, grad_values = attend_back(
        queries, key_rows, value_rows, mixed, log_total, grad_mixed, allowed
    )
    grad_queries = rotate(grad_queries, cosine, -sine)
    grad_keys = rotate(grad_keys, cosine, -sine)
    bias_terms = jnp.stack([jnp.sum(g, axis=0) for g in (grad_queries, grad_keys, grad_values)])
    attn_in_t = turned(attn_in, order)
    grad_proj = [g.astype(BF16).reshape(length, -1) for g in (grad_queries, grad_keys, grad_values)]
    v_grad = scatter_product(grid, attn_in_t, grad_proj[2])
    q_grad = scatter_product(grid, attn_in_t, grad_proj[0])
    k_grad = scatter_product(grid, attn_in_t, grad_proj[1])
    grad_attn_in = collect(
        times_transposed(grad_proj[0], w_q) + times_transposed(grad_proj[1], w_k) + times_transposed(grad_proj[2], w_v)
    )
    _, normed_one, inv_one = norm_forward(resid, gains[0], shifts[0])
    grad_norm_one, gain_one, shift_one = norm_backward(grad_attn_in, normed_one, inv_one, gains[0])
    input_grad = (grad_two + grad_norm_one).astype(BF16)

    gate_up_grad = jnp.stack([gate_grad, up_grad], axis=1)[None]
    norm_terms = jnp.stack([gain_one, gain_two, shift_one, shift_two])
    norm_terms = jnp.swapaxes(norm_terms.reshape(4, count, block), 0, 1).reshape(count, 4 * block)
    bias_terms = jnp.transpose(bias_terms.reshape(3, heads, count, piece), (2, 0, 1, 3)).reshape(count, -1)
    terms = jnp.concatenate([norm_terms, bias_terms], axis=1)
    n_terms = terms.shape[1]
    term_rows = 8 * (-(-n_terms // (8 * 128)))
    terms = jnp.pad(terms, ((0, 0), (0, term_rows * 128 - n_terms))).reshape(count * term_rows, 128)
    terms = lax.psum(terms, "fsdp")
    terms = lax.dynamic_slice_in_dim(terms, lax.axis_index("fsdp") * term_rows, term_rows, 0).reshape(-1)
    norm_part = terms[: 4 * block].reshape(4, block)
    norm_part = norm_part + other(norm_part)
    bias_part = terms[4 * block : n_terms].reshape(3, heads, piece)
    return (
        block_output,
        input_grad,
        norm_part[None, 0:2],
        norm_part[None, 2:4],
        jnp.stack([q_grad, k_grad, v_grad], axis=1)[None],
        bias_part[None],
        out_grad.T[None],
        gate_up_grad,
        down_grad.T[None],
    )


def solution(mesh):
    placed = (
        P(("fsdp", "tp"), None),
        P("fsdp", None),
        P(("fsdp", "tp"), None),
        P(None, None, "fsdp"),
        P(None, None, "fsdp"),
        P(None, "fsdp", None, "tp"),
        P(None, None, "tp", "fsdp"),
        P(None, "tp", "fsdp"),
        P(None, "fsdp", None, "tp"),
        P(None, "tp", "fsdp"),
    )

    def body(*args):
        return shards(Grid(mesh), *args)

    return jax.shard_map(
        body,
        mesh=mesh,
        in_specs=placed,
        out_specs=(
            P(("fsdp", "tp"), None),
            P(("fsdp", "tp"), None),
            P(None, None, "fsdp"),
            P(None, None, "fsdp"),
            P(None, "fsdp", None, "tp"),
            P(None, None, "tp", "fsdp"),
            P(None, "tp", "fsdp"),
            P(None, "fsdp", None, "tp"),
            P(None, "tp", "fsdp"),
        ),
        check_vma=False,
    )
```

```python
import jax
import jax.numpy as jnp
from jax import lax
from jax.experimental import pallas as pl
from jax.experimental.pallas import tpu as pltpu
from jax.sharding import PartitionSpec as P


HEAD = 64
ROTARY = 16

EPS = 1e-05
NEG = -1e30
SCALE = 0.125
ROPE_BASE = 10000.0

BF16 = jnp.bfloat16
F32 = jnp.float32


def times(left, right):
    return lax.dot_general(left, right, (((1,), (0,)), ((), ())), preferred_element_type=F32)


def times_transposed(left, right):
    return lax.dot_general(left, right, (((1,), (1,)), ((), ())), preferred_element_type=F32)


class Grid:
    def __init__(self, mesh):
        self.count = mesh.shape["fsdp"]
        column = list(mesh.devices[:, 0])
        spots = [tuple(d.coords) for d in column]
        self.cores = 2 if self.count > 1 and spots[0] == spots[1] else 1
        run = 1
        while run < self.count and spots[run][2] == spots[0][2]:
            run += 1
        self.slow = self.count // run
        self.mid = run // self.cores

    def place(self, slow, mid, core):
        return ((slow % self.slow) * self.mid + mid % self.mid) * self.cores + core % self.cores

    def moves(self, slow=0, mid=0, core=0):
        return [
            (self.place(s, m, c), self.place(s + slow, m + mid, c + core))
            for s in range(self.slow)
            for m in range(self.mid)
            for c in range(self.cores)
        ]

    def shift(self, rows, **by):
        return lax.ppermute(rows, "fsdp", self.moves(**by))

    def across(self, slow, step):
        return slow ^ step if self.slow == 4 else (slow + step) % self.slow

    def cross(self, rows, step, ends=True, inner=True):
        moves = []
        for s in range(self.slow):
            if ends if s in (0, self.slow - 1) else inner:
                moves += [
                    (self.place(s, m, c), self.place(self.across(s, step), m, c))
                    for m in range(self.mid)
                    for c in range(self.cores)
                ]
        return lax.ppermute(rows, "fsdp", moves)

    def order(self):
        here = lax.axis_index("fsdp")
        core = here % self.cores
        mid = (here // self.cores) % self.mid
        slow = here // (self.cores * self.mid)
        step = jnp.arange(self.count, dtype=jnp.int32)
        core = (core + step // (self.mid * self.slow)) % self.cores
        mid = (mid + (step // self.slow) % self.mid) % self.mid
        slow = self.across(slow, step % self.slow)
        return ((slow * self.mid + mid) * self.cores + core).astype(jnp.int32)


def flip_kernel(order_ref, rows_ref, out_ref):
    count = order_ref.shape[0]
    block = rows_ref.shape[1] // count

    def move(j, carry):
        start = pl.multiple_of(order_ref[j] * block, block)
        out_ref[pl.ds(pl.multiple_of(j * block, block), block), :] = rows_ref[:, pl.ds(start, block)].T
        return carry

    lax.fori_loop(0, count, move, 0)


def turned(rows, order):
    tokens, width = rows.shape
    count = order.shape[0]
    block = width // count
    if block % 128:
        return rows.T.reshape(count, block, tokens)[order].reshape(width, tokens)
    return pl.pallas_call(
        flip_kernel,
        grid_spec=pltpu.PrefetchScalarGridSpec(
            num_scalar_prefetch=1,
            grid=(1,),
            in_specs=[pl.BlockSpec((tokens, width), lambda i, order: (0, 0))],
            out_specs=pl.BlockSpec((width, tokens), lambda i, order: (0, 0)),
        ),
        out_shape=jax.ShapeDtypeStruct((width, tokens), rows.dtype),
    )(order, rows)


def scatter_product(grid, left, right, relay=False):
    block = left.shape[0] // grid.count
    per_mid = block * grid.slow
    per_core = per_mid * grid.mid
    from_core = []
    for c in range(1, grid.cores):
        out = times(left[c * per_core : (c + 1) * per_core], right).astype(BF16)
        from_core.append(grid.shift(out, core=c))
    from_mid = []
    for m in range(1, grid.mid):
        part = times(left[m * per_mid : (m + 1) * per_mid], right)
        for got in from_core:
            part = part + got[m * per_mid : (m + 1) * per_mid].astype(F32)
        part = part.astype(BF16)
        from_mid.append(grid.shift(part, mid=m))

    def part_of(span):
        part = times(left[span], right)
        for got in from_core + from_mid:
            part = part + got[span].astype(F32)
        return part

    total = part_of(slice(0, block))
    from_slow = []
    if relay and grid.slow == 4:
        mine = part_of(slice(block, 4 * block)).astype(BF16)
        got = grid.cross(mine, 1, inner=False)
        near, far, over = (slice(i * block, (i + 1) * block) for i in range(3))
        from_slow.append(got[near])
        sums = {
            1: mine[near],
            2: (mine[far].astype(F32) + got[over].astype(F32)).astype(BF16),
            3: (mine[over].astype(F32) + got[far].astype(F32)).astype(BF16),
        }
        from_slow += [grid.cross(rows, s, ends=False) for s, rows in sums.items()]
    else:
        for s in range(1, grid.slow):
            part = part_of(slice(s * block, (s + 1) * block)).astype(BF16)
            from_slow.append(grid.cross(part, s))
    for got in from_slow:
        total = total + got.astype(F32)
    return total


def scatter_rows(grid, rows):
    per_core = grid.mid * grid.slow
    total = rows[:per_core]
    for c in range(1, grid.cores):
        total = total + grid.shift(rows[c * per_core : (c + 1) * per_core], core=c)
    rows, total = total, total[: grid.slow]
    for m in range(1, grid.mid):
        total = total + grid.shift(rows[m * grid.slow : (m + 1) * grid.slow], mid=m)
    rows, total = total, total[0]
    for s in range(1, grid.slow):
        total = total + grid.cross(rows[s], s)
    return total


def other(rows):
    return lax.ppermute(rows, "tp", [(0, 1), (1, 0)])


def pair(rows):
    return jnp.concatenate([rows, other(rows)], axis=0)


def collect(term):
    half = term.shape[0] // 2
    return term[:half] + other(term[half:].astype(BF16)).astype(F32)


def norm_forward(rows, gain, shift):
    center = rows - jnp.mean(rows, axis=1, keepdims=True)
    inv_std = lax.rsqrt(jnp.mean(center * center, axis=1, keepdims=True) + EPS)
    normed = center * inv_std
    return (normed * gain + shift, normed, inv_std)


def norm_backward(grad_out, normed, inv_std, gain):
    scaled = grad_out * gain
    grad_in = inv_std * (
        scaled
        - jnp.mean(scaled, axis=1, keepdims=True)
        - normed * jnp.mean(scaled * normed, axis=1, keepdims=True)
    )
    return (grad_in, jnp.sum(grad_out * normed, axis=0), jnp.sum(grad_out, axis=0))


def rope_tables(position):
    half = ROTARY // 2
    inverse = ROPE_BASE ** (-jnp.arange(half).astype(F32) * 2.0 / ROTARY)
    angles = position.astype(F32)[:, None] * inverse[None, :]
    return (jnp.cos(angles)[:, None, :], jnp.sin(angles)[:, None, :])


def rotate(values, cosine, sine):
    half = ROTARY // 2
    first = values[..., :half]
    second = values[..., half:ROTARY]
    return jnp.concatenate(
        [first * cosine - second * sine, second * cosine + first * sine, values[..., ROTARY:]],
        axis=-1,
    )


def masked_scores(queries, key_rows, allowed):
    scores = jnp.einsum("qhd,khd->hqk", queries, key_rows, preferred_element_type=F32) * SCALE
    return jnp.where(allowed, scores, NEG)


def attend(queries, key_rows, value_rows, allowed):
    scores = masked_scores(queries, key_rows, allowed)
    top = jnp.max(scores, axis=-1, keepdims=True)
    log_total = top + jnp.log(jnp.sum(jnp.exp(scores - top), axis=-1, keepdims=True))
    probs = jnp.exp(scores - log_total).astype(BF16)
    mixed = jnp.einsum("hqk,khd->qhd", probs, value_rows, preferred_element_type=F32).astype(BF16)
    return (mixed, log_total)


def attend_back(queries, key_rows, value_rows, mixed, log_total, grad_mixed, allowed):
    scores = masked_scores(queries, key_rows, allowed)
    probs = jnp.exp(scores - log_total)
    grad_values = jnp.einsum("hqk,qhd->khd", probs.astype(BF16), grad_mixed, preferred_element_type=F32)
    grad_probs = jnp.einsum("qhd,khd->hqk", grad_mixed, value_rows, preferred_element_type=F32)
    delta = jnp.sum(grad_mixed.astype(F32) * mixed.astype(F32), axis=-1)
    delta = jnp.transpose(delta, (1, 0))[..., None]
    grad_scores = (probs * (grad_probs - delta) * SCALE).astype(BF16)
    grad_queries = jnp.einsum("hqk,khd->qhd", grad_scores, key_rows, preferred_element_type=F32)
    grad_keys = jnp.einsum("hqk,qhd->khd", grad_scores, queries, preferred_element_type=F32)
    return (grad_queries, grad_keys, grad_values)


def shards(
    grid,
    block_input,
    segments,
    cotangent,
    norm_gain,
    norm_shift,
    qkv_weight,
    qkv_bias,
    out_weight,
    gate_up_weight,
    down_weight,
):
    count = grid.count
    mine = block_input.shape[0]
    length = segments.shape[1]
    width = block_input.shape[1]
    block = width // count
    wide = qkv_weight.shape[3]
    heads = qkv_bias.shape[2]
    piece = qkv_bias.shape[3]
    turn = lax.axis_index("tp")

    small = jnp.concatenate(
        [norm_gain.reshape(-1), norm_shift.reshape(-1), qkv_bias.reshape(-1)]
    )
    n_small = small.shape[0]
    small_rows = 16 * (-(-n_small // (16 * wide)))
    small = jnp.pad(small, (0, small_rows * wide - n_small)).reshape(small_rows, wide)
    pack = jnp.concatenate(
        [qkv_weight[0, :, 0], qkv_weight[0, :, 1], qkv_weight[0, :, 2], out_weight[0].T, small], axis=0
    )
    packs = lax.all_gather(pack, "fsdp", axis=0)
    gate_up_all = lax.all_gather(jnp.swapaxes(gate_up_weight[0], 0, 1), "fsdp", axis=1, tiled=True)
    w_down = lax.all_gather(down_weight[0], "fsdp", axis=1, tiled=True)

    w_q, w_k, w_v, w_out_t = (
        packs[:, i * block : (i + 1) * block].reshape(width, wide) for i in range(4)
    )
    small_all = packs[:, 4 * block :].reshape(count, -1)
    gains = jnp.swapaxes(small_all[:, : 2 * block].reshape(count, 2, block), 0, 1).reshape(2, width)
    shifts = jnp.swapaxes(small_all[:, 2 * block : 4 * block].reshape(count, 2, block), 0, 1).reshape(2, width)
    bias = small_all[:, 4 * block : 4 * block + 3 * heads * piece].reshape(count, 3, heads, piece)
    bias = jnp.transpose(bias, (1, 2, 0, 3)).reshape(3, heads * HEAD).astype(F32)
    gains = gains.astype(F32)
    shifts = shifts.astype(F32)
    w_gate = gate_up_all[0]
    w_up = gate_up_all[1]

    position = (jnp.arange(length, dtype=jnp.int32) + turn * mine) % length
    cosine, sine = rope_tables(position)
    seg_row = segments[0]
    seg_row = jnp.where(turn == 0, seg_row, jnp.roll(seg_row, mine))
    allowed = (seg_row[:, None] == seg_row[None, :]) & (position[:, None] >= position[None, :])

    order = grid.order()
    down_cot = pair(cotangent)
    down_cot_t = turned(down_cot, order)
    rows_all = pair(block_input).astype(F32)
    resid = block_input.astype(F32)

    first_norm, _, _ = norm_forward(rows_all, gains[0], shifts[0])
    attn_in = first_norm.astype(BF16)
    queries = (times(attn_in, w_q) + bias[0]).reshape(length, heads, HEAD)
    key_rows = (times(attn_in, w_k) + bias[1]).reshape(length, heads, HEAD)
    value_rows = (times(attn_in, w_v) + bias[2]).reshape(length, heads, HEAD)
    queries = rotate(queries, cosine, sine).astype(BF16)
    key_rows = rotate(key_rows, cosine, sine).astype(BF16)
    value_rows = value_rows.astype(BF16)
    mixed, log_total = attend(queries, key_rows, value_rows, allowed)
    mixed_flat = mixed.reshape(length, -1)
    resid_two = resid + collect(times_transposed(mixed_flat, w_out_t))
    second_norm, normed_two, inv_two = norm_forward(resid_two, gains[1], shifts[1])
    mlp_in = pair(second_norm.astype(BF16))
    gate = times(mlp_in, w_gate)
    upper = times(mlp_in, w_up)
    sigma = jax.nn.sigmoid(gate)
    hidden = (gate * sigma * upper).astype(BF16)
    gate, upper, hidden = lax.optimization_barrier((gate, upper, hidden))
    sigma = jax.nn.sigmoid(gate)
    down_grad = scatter_product(grid, down_cot_t, hidden, relay=True)

    grad_three = cotangent.astype(F32)
    grad_hidden = times_transposed(down_cot, w_down)
    grad_gate = (grad_hidden * upper * sigma * (1.0 + gate * (1.0 - sigma))).astype(BF16)
    grad_up = (grad_hidden * gate * sigma).astype(BF16)
    mlp_in_t = turned(mlp_in, order)
    half = grad_gate.shape[1] // 2
    gate_grad, up_grad = (
        jnp.concatenate(
            [
                scatter_product(grid, mlp_in_t, grad[:, :half], relay=True),
                scatter_product(grid, mlp_in_t, grad[:, half:], relay=True),
            ],
            axis=1,
        )
        for grad in (grad_gate, grad_up)
    )
    grad_mlp_in = collect(times_transposed(grad_gate, w_gate) + times_transposed(grad_up, w_up))
    grad_norm_two, gain_two, shift_two = norm_backward(grad_mlp_in, normed_two, inv_two, gains[1])
    grad_two = grad_three + grad_norm_two
    attn_cot = pair(grad_two.astype(BF16))
    attn_cot, hidden_late = lax.optimization_barrier((attn_cot, hidden))
    resid_three = resid_two + collect(times(hidden_late, w_down))
    block_output = resid_three.astype(BF16)
    grad_mixed = times(attn_cot, w_out_t).astype(BF16).reshape(mixed.shape)
    out_grad = scatter_product(grid, turned(attn_cot, order), mixed_flat)
    grad_queries, grad_keys, grad_values = attend_back(
        queries, key_rows, value_rows, mixed, log_total, grad_mixed, allowed
    )
    grad_queries = rotate(grad_queries, cosine, -sine)
    grad_keys = rotate(grad_keys, cosine, -sine)
    bias_terms = jnp.stack([jnp.sum(g, axis=0) for g in (grad_queries, grad_keys, grad_values)])
    attn_in_t = turned(attn_in, order)
    grad_proj = [g.astype(BF16).reshape(length, -1) for g in (grad_queries, grad_keys, grad_values)]
    v_grad = scatter_product(grid, attn_in_t, grad_proj[2])
    q_grad = scatter_product(grid, attn_in_t, grad_proj[0])
    k_grad = scatter_product(grid, attn_in_t, grad_proj[1])
    grad_attn_in = collect(
        times_transposed(grad_proj[0], w_q) + times_transposed(grad_proj[1], w_k) + times_transposed(grad_proj[2], w_v)
    )
    _, normed_one, inv_one = norm_forward(resid, gains[0], shifts[0])
    grad_norm_one, gain_one, shift_one = norm_backward(grad_attn_in, normed_one, inv_one, gains[0])
    input_grad = (grad_two + grad_norm_one).astype(BF16)

    gate_up_grad = jnp.stack([gate_grad, up_grad], axis=1)[None]
    norm_terms = jnp.stack([gain_one, gain_two, shift_one, shift_two])
    norm_terms = jnp.swapaxes(norm_terms.reshape(4, count, block), 0, 1).reshape(count, 4 * block)
    bias_terms = jnp.transpose(bias_terms.reshape(3, heads, count, piece), (2, 0, 1, 3)).reshape(count, -1)
    terms = scatter_rows(grid, jnp.concatenate([norm_terms, bias_terms], axis=1)[order])
    norm_part = terms[: 4 * block].reshape(4, block)
    norm_part = norm_part + other(norm_part)
    bias_part = terms[4 * block :].reshape(3, heads, piece)
    return (
        block_output,
        input_grad,
        norm_part[None, 0:2],
        norm_part[None, 2:4],
        jnp.stack([q_grad, k_grad, v_grad], axis=1)[None],
        bias_part[None],
        out_grad.T[None],
        gate_up_grad,
        down_grad.T[None],
    )


def solution(mesh):
    placed = (
        P(("fsdp", "tp"), None),
        P("fsdp", None),
        P(("fsdp", "tp"), None),
        P(None, None, "fsdp"),
        P(None, None, "fsdp"),
        P(None, "fsdp", None, "tp"),
        P(None, None, "tp", "fsdp"),
        P(None, "tp", "fsdp"),
        P(None, "fsdp", None, "tp"),
        P(None, "tp", "fsdp"),
    )

    def body(*args):
        return shards(Grid(mesh), *args)

    return jax.shard_map(
        body,
        mesh=mesh,
        in_specs=placed,
        out_specs=(
            P(("fsdp", "tp"), None),
            P(("fsdp", "tp"), None),
            P(None, None, "fsdp"),
            P(None, None, "fsdp"),
            P(None, "fsdp", None, "tp"),
            P(None, None, "tp", "fsdp"),
            P(None, "tp", "fsdp"),
            P(None, "fsdp", None, "tp"),
            P(None, "tp", "fsdp"),
        ),
        check_vma=False,
    )
```

```python
import jax
import jax.numpy as jnp
from jax import lax
from jax.experimental import pallas as pl
from jax.experimental.pallas import tpu as pltpu
from jax.sharding import PartitionSpec as P


HEAD = 64
ROTARY = 16

EPS = 1e-05
NEG = -1e30
SCALE = 0.125
ROPE_BASE = 10000.0

BF16 = jnp.bfloat16
F32 = jnp.float32


def times(left, right):
    return lax.dot_general(left, right, (((1,), (0,)), ((), ())), preferred_element_type=F32)


def times_transposed(left, right):
    return lax.dot_general(left, right, (((1,), (1,)), ((), ())), preferred_element_type=F32)


class Grid:
    def __init__(self, mesh):
        self.count = mesh.shape["fsdp"]
        column = list(mesh.devices[:, 0])
        spots = [tuple(d.coords) for d in column]
        self.cores = 2 if self.count > 1 and spots[0] == spots[1] else 1
        run = 1
        while run < self.count and spots[run][2] == spots[0][2]:
            run += 1
        self.slow = self.count // run
        self.mid = run // self.cores

    def place(self, slow, mid, core):
        return ((slow % self.slow) * self.mid + mid % self.mid) * self.cores + core % self.cores

    def moves(self, slow=0, mid=0, core=0):
        return [
            (self.place(s, m, c), self.place(s + slow, m + mid, c + core))
            for s in range(self.slow)
            for m in range(self.mid)
            for c in range(self.cores)
        ]

    def shift(self, rows, **by):
        return lax.ppermute(rows, "fsdp", self.moves(**by))

    def across(self, slow, step):
        return slow ^ step if self.slow == 4 else (slow + step) % self.slow

    def cross(self, rows, step, ends=True, inner=True):
        moves = []
        for s in range(self.slow):
            if ends if s in (0, self.slow - 1) else inner:
                moves += [
                    (self.place(s, m, c), self.place(self.across(s, step), m, c))
                    for m in range(self.mid)
                    for c in range(self.cores)
                ]
        return lax.ppermute(rows, "fsdp", moves)

    def order(self):
        here = lax.axis_index("fsdp")
        core = here % self.cores
        mid = (here // self.cores) % self.mid
        slow = here // (self.cores * self.mid)
        step = jnp.arange(self.count, dtype=jnp.int32)
        core = (core + step // (self.mid * self.slow)) % self.cores
        mid = (mid + (step // self.slow) % self.mid) % self.mid
        slow = self.across(slow, step % self.slow)
        return ((slow * self.mid + mid) * self.cores + core).astype(jnp.int32)


def flip_kernel(order_ref, rows_ref, out_ref):
    count = order_ref.shape[0]
    block = rows_ref.shape[1] // count

    def move(j, carry):
        start = pl.multiple_of(order_ref[j] * block, block)
        out_ref[pl.ds(pl.multiple_of(j * block, block), block), :] = rows_ref[:, pl.ds(start, block)].T
        return carry

    lax.fori_loop(0, count, move, 0)


def turned(rows, order):
    tokens, width = rows.shape
    count = order.shape[0]
    block = width // count
    if block % 128:
        return rows.T.reshape(count, block, tokens)[order].reshape(width, tokens)
    return pl.pallas_call(
        flip_kernel,
        grid_spec=pltpu.PrefetchScalarGridSpec(
            num_scalar_prefetch=1,
            grid=(1,),
            in_specs=[pl.BlockSpec((tokens, width), lambda i, order: (0, 0))],
            out_specs=pl.BlockSpec((width, tokens), lambda i, order: (0, 0)),
        ),
        out_shape=jax.ShapeDtypeStruct((width, tokens), rows.dtype),
    )(order, rows)


def scatter_product(grid, left, right, relay=False):
    block = left.shape[0] // grid.count
    per_mid = block * grid.slow
    per_core = per_mid * grid.mid
    from_core = []
    for c in range(1, grid.cores):
        out = times(left[c * per_core : (c + 1) * per_core], right).astype(BF16)
        from_core.append(grid.shift(out, core=c))
    from_mid = []
    for m in range(1, grid.mid):
        part = times(left[m * per_mid : (m + 1) * per_mid], right)
        for got in from_core:
            part = part + got[m * per_mid : (m + 1) * per_mid].astype(F32)
        part = part.astype(BF16)
        from_mid.append(grid.shift(part, mid=m))

    def part_of(span):
        part = times(left[span], right)
        for got in from_core + from_mid:
            part = part + got[span].astype(F32)
        return part

    total = part_of(slice(0, block))
    from_slow = []
    if relay and grid.slow == 4:
        mine = part_of(slice(block, 4 * block)).astype(BF16)
        got = grid.cross(mine, 1, inner=False)
        near, far, over = (slice(i * block, (i + 1) * block) for i in range(3))
        from_slow.append(got[near])
        sums = {
            1: mine[near],
            2: (mine[far].astype(F32) + got[over].astype(F32)).astype(BF16),
            3: (mine[over].astype(F32) + got[far].astype(F32)).astype(BF16),
        }
        from_slow += [grid.cross(rows, s, ends=False) for s, rows in sums.items()]
    else:
        for s in range(1, grid.slow):
            part = part_of(slice(s * block, (s + 1) * block)).astype(BF16)
            from_slow.append(grid.cross(part, s))
    for got in from_slow:
        total = total + got.astype(F32)
    return total


def scatter_rows(grid, rows):
    per_core = grid.mid * grid.slow
    total = rows[:per_core]
    for c in range(1, grid.cores):
        total = total + grid.shift(rows[c * per_core : (c + 1) * per_core], core=c)
    rows, total = total, total[: grid.slow]
    for m in range(1, grid.mid):
        total = total + grid.shift(rows[m * grid.slow : (m + 1) * grid.slow], mid=m)
    rows, total = total, total[0]
    for s in range(1, grid.slow):
        total = total + grid.cross(rows[s], s)
    return total


def other(rows):
    return lax.ppermute(rows, "tp", [(0, 1), (1, 0)])


def pair(rows):
    return jnp.concatenate([rows, other(rows)], axis=0)


def collect(term):
    half = term.shape[0] // 2
    return term[:half] + other(term[half:].astype(BF16)).astype(F32)


def norm_forward(rows, gain, shift):
    center = rows - jnp.mean(rows, axis=1, keepdims=True)
    inv_std = lax.rsqrt(jnp.mean(center * center, axis=1, keepdims=True) + EPS)
    normed = center * inv_std
    return (normed * gain + shift, normed, inv_std)


def norm_backward(grad_out, normed, inv_std, gain):
    scaled = grad_out * gain
    grad_in = inv_std * (
        scaled
        - jnp.mean(scaled, axis=1, keepdims=True)
        - normed * jnp.mean(scaled * normed, axis=1, keepdims=True)
    )
    return (grad_in, jnp.sum(grad_out * normed, axis=0), jnp.sum(grad_out, axis=0))


def rope_tables(position):
    half = ROTARY // 2
    inverse = ROPE_BASE ** (-jnp.arange(half).astype(F32) * 2.0 / ROTARY)
    angles = position.astype(F32)[:, None] * inverse[None, :]
    return (jnp.cos(angles)[:, None, :], jnp.sin(angles)[:, None, :])


def rotate(values, cosine, sine):
    half = ROTARY // 2
    first = values[..., :half]
    second = values[..., half:ROTARY]
    return jnp.concatenate(
        [first * cosine - second * sine, second * cosine + first * sine, values[..., ROTARY:]],
        axis=-1,
    )


def masked_scores(queries, key_rows, allowed):
    scores = jnp.einsum("qhd,khd->hqk", queries, key_rows, preferred_element_type=F32) * SCALE
    return jnp.where(allowed, scores, NEG)


def attend(queries, key_rows, value_rows, allowed):
    scores = masked_scores(queries, key_rows, allowed)
    top = jnp.max(scores, axis=-1, keepdims=True)
    log_total = top + jnp.log(jnp.sum(jnp.exp(scores - top), axis=-1, keepdims=True))
    probs = jnp.exp(scores - log_total).astype(BF16)
    mixed = jnp.einsum("hqk,khd->qhd", probs, value_rows, preferred_element_type=F32).astype(BF16)
    return (mixed, log_total)


def attend_back(queries, key_rows, value_rows, mixed, log_total, grad_mixed, allowed):
    scores = masked_scores(queries, key_rows, allowed)
    probs = jnp.exp(scores - log_total)
    grad_values = jnp.einsum("hqk,qhd->khd", probs.astype(BF16), grad_mixed, preferred_element_type=F32)
    grad_probs = jnp.einsum("qhd,khd->hqk", grad_mixed, value_rows, preferred_element_type=F32)
    delta = jnp.sum(grad_mixed.astype(F32) * mixed.astype(F32), axis=-1)
    delta = jnp.transpose(delta, (1, 0))[..., None]
    grad_scores = (probs * (grad_probs - delta) * SCALE).astype(BF16)
    grad_queries = jnp.einsum("hqk,khd->qhd", grad_scores, key_rows, preferred_element_type=F32)
    grad_keys = jnp.einsum("hqk,qhd->khd", grad_scores, queries, preferred_element_type=F32)
    return (grad_queries, grad_keys, grad_values)


def shards(
    grid,
    block_input,
    segments,
    cotangent,
    norm_gain,
    norm_shift,
    qkv_weight,
    qkv_bias,
    out_weight,
    gate_up_weight,
    down_weight,
):
    count = grid.count
    mine = block_input.shape[0]
    length = segments.shape[1]
    width = block_input.shape[1]
    block = width // count
    wide = qkv_weight.shape[3]
    heads = qkv_bias.shape[2]
    piece = qkv_bias.shape[3]
    turn = lax.axis_index("tp")

    small = jnp.concatenate(
        [norm_gain.reshape(-1), norm_shift.reshape(-1), qkv_bias.reshape(-1)]
    )
    n_small = small.shape[0]
    small_rows = 16 * (-(-n_small // (16 * wide)))
    small = jnp.pad(small, (0, small_rows * wide - n_small)).reshape(small_rows, wide)
    pack = jnp.concatenate(
        [qkv_weight[0, :, 0], qkv_weight[0, :, 1], qkv_weight[0, :, 2], out_weight[0].T, small], axis=0
    )
    packs = lax.all_gather(pack, "fsdp", axis=0)
    mlp_pack = jnp.stack([gate_up_weight[0, :, 0], gate_up_weight[0, :, 1], down_weight[0].T])
    mlp_all = lax.all_gather(mlp_pack, "fsdp", axis=1, tiled=True)

    w_q, w_k, w_v, w_out_t = (
        packs[:, i * block : (i + 1) * block].reshape(width, wide) for i in range(4)
    )
    small_all = packs[:, 4 * block :].reshape(count, -1)
    gains = jnp.swapaxes(small_all[:, : 2 * block].reshape(count, 2, block), 0, 1).reshape(2, width)
    shifts = jnp.swapaxes(small_all[:, 2 * block : 4 * block].reshape(count, 2, block), 0, 1).reshape(2, width)
    bias = small_all[:, 4 * block : 4 * block + 3 * heads * piece].reshape(count, 3, heads, piece)
    bias = jnp.transpose(bias, (1, 2, 0, 3)).reshape(3, heads * HEAD).astype(F32)
    gains = gains.astype(F32)
    shifts = shifts.astype(F32)
    w_gate, w_up, w_down_t = mlp_all[0], mlp_all[1], mlp_all[2]

    position = (jnp.arange(length, dtype=jnp.int32) + turn * mine) % length
    cosine, sine = rope_tables(position)
    seg_row = segments[0]
    seg_row = jnp.where(turn == 0, seg_row, jnp.roll(seg_row, mine))
    allowed = (seg_row[:, None] == seg_row[None, :]) & (position[:, None] >= position[None, :])

    order = grid.order()
    down_cot = pair(cotangent)
    down_cot_t = turned(down_cot, order)
    rows_all = pair(block_input).astype(F32)
    resid = block_input.astype(F32)

    first_norm, _, _ = norm_forward(rows_all, gains[0], shifts[0])
    attn_in = first_norm.astype(BF16)
    queries = (times(attn_in, w_q) + bias[0]).reshape(length, heads, HEAD)
    key_rows = (times(attn_in, w_k) + bias[1]).reshape(length, heads, HEAD)
    value_rows = (times(attn_in, w_v) + bias[2]).reshape(length, heads, HEAD)
    queries = rotate(queries, cosine, sine).astype(BF16)
    key_rows = rotate(key_rows, cosine, sine).astype(BF16)
    value_rows = value_rows.astype(BF16)
    mixed, log_total = attend(queries, key_rows, value_rows, allowed)
    mixed_flat = mixed.reshape(length, -1)
    resid_two = resid + collect(times_transposed(mixed_flat, w_out_t))
    second_norm, normed_two, inv_two = norm_forward(resid_two, gains[1], shifts[1])
    mlp_in = pair(second_norm.astype(BF16))
    gate = times(mlp_in, w_gate)
    upper = times(mlp_in, w_up)
    sigma = jax.nn.sigmoid(gate)
    hidden = (gate * sigma * upper).astype(BF16)
    gate, upper, hidden = lax.optimization_barrier((gate, upper, hidden))
    sigma = jax.nn.sigmoid(gate)
    down_grad = scatter_product(grid, down_cot_t, hidden, relay=True)

    grad_three = cotangent.astype(F32)
    grad_hidden = times(down_cot, w_down_t)
    grad_gate = (grad_hidden * upper * sigma * (1.0 + gate * (1.0 - sigma))).astype(BF16)
    grad_up = (grad_hidden * gate * sigma).astype(BF16)
    mlp_in_t = turned(mlp_in, order)
    half = grad_gate.shape[1] // 2
    gate_grad, up_grad = (
        jnp.concatenate(
            [
                scatter_product(grid, mlp_in_t, grad[:, :half], relay=True),
                scatter_product(grid, mlp_in_t, grad[:, half:], relay=True),
            ],
            axis=1,
        )
        for grad in (grad_gate, grad_up)
    )
    grad_mlp_in = collect(times_transposed(grad_gate, w_gate) + times_transposed(grad_up, w_up))
    grad_norm_two, gain_two, shift_two = norm_backward(grad_mlp_in, normed_two, inv_two, gains[1])
    grad_two = grad_three + grad_norm_two
    attn_cot = pair(grad_two.astype(BF16))
    attn_cot, hidden_late = lax.optimization_barrier((attn_cot, hidden))
    resid_three = resid_two + collect(times_transposed(hidden_late, w_down_t))
    block_output = resid_three.astype(BF16)
    grad_mixed = times(attn_cot, w_out_t).astype(BF16).reshape(mixed.shape)
    out_grad = scatter_product(grid, turned(attn_cot, order), mixed_flat)
    grad_queries, grad_keys, grad_values = attend_back(
        queries, key_rows, value_rows, mixed, log_total, grad_mixed, allowed
    )
    grad_queries = rotate(grad_queries, cosine, -sine)
    grad_keys = rotate(grad_keys, cosine, -sine)
    bias_terms = jnp.stack([jnp.sum(g, axis=0) for g in (grad_queries, grad_keys, grad_values)])
    attn_in_t = turned(attn_in, order)
    grad_proj = [g.astype(BF16).reshape(length, -1) for g in (grad_queries, grad_keys, grad_values)]
    v_grad = scatter_product(grid, attn_in_t, grad_proj[2])
    q_grad = scatter_product(grid, attn_in_t, grad_proj[0])
    k_grad = scatter_product(grid, attn_in_t, grad_proj[1])
    grad_attn_in = collect(
        times_transposed(grad_proj[0], w_q)
        + times_transposed(grad_proj[1], w_k)
        + times_transposed(grad_proj[2], w_v),
    )
    _, normed_one, inv_one = norm_forward(resid, gains[0], shifts[0])
    grad_norm_one, gain_one, shift_one = norm_backward(grad_attn_in, normed_one, inv_one, gains[0])
    input_grad = (grad_two + grad_norm_one).astype(BF16)

    gate_up_grad = jnp.stack([gate_grad, up_grad], axis=1)[None]
    norm_terms = jnp.stack([gain_one, gain_two, shift_one, shift_two])
    norm_terms = jnp.swapaxes(norm_terms.reshape(4, count, block), 0, 1).reshape(count, 4 * block)
    bias_terms = jnp.transpose(bias_terms.reshape(3, heads, count, piece), (2, 0, 1, 3)).reshape(count, -1)
    terms = scatter_rows(grid, jnp.concatenate([norm_terms, bias_terms], axis=1)[order])
    norm_part = terms[: 4 * block].reshape(4, block)
    norm_part = norm_part + other(norm_part)
    bias_part = terms[4 * block :].reshape(3, heads, piece)
    return (
        block_output,
        input_grad,
        norm_part[None, 0:2],
        norm_part[None, 2:4],
        jnp.stack([q_grad, k_grad, v_grad], axis=1)[None],
        bias_part[None],
        out_grad.T[None],
        gate_up_grad,
        down_grad.T[None],
    )


def solution(mesh):
    placed = (
        P(("fsdp", "tp"), None),
        P("fsdp", None),
        P(("fsdp", "tp"), None),
        P(None, None, "fsdp"),
        P(None, None, "fsdp"),
        P(None, "fsdp", None, "tp"),
        P(None, None, "tp", "fsdp"),
        P(None, "tp", "fsdp"),
        P(None, "fsdp", None, "tp"),
        P(None, "tp", "fsdp"),
    )

    def body(*args):
        return shards(Grid(mesh), *args)

    return jax.shard_map(
        body,
        mesh=mesh,
        in_specs=placed,
        out_specs=(
            P(("fsdp", "tp"), None),
            P(("fsdp", "tp"), None),
            P(None, None, "fsdp"),
            P(None, None, "fsdp"),
            P(None, "fsdp", None, "tp"),
            P(None, None, "tp", "fsdp"),
            P(None, "tp", "fsdp"),
            P(None, "fsdp", None, "tp"),
            P(None, "tp", "fsdp"),
        ),
        check_vma=False,
    )
```

```python
import jax
import jax.numpy as jnp
from jax import lax
from jax.experimental import pallas as pl
from jax.experimental.pallas import tpu as pltpu
from jax.sharding import PartitionSpec as P


HEAD = 64
ROTARY = 16

EPS = 1e-05
NEG = -1e30
SCALE = 0.125
ROPE_BASE = 10000.0

BF16 = jnp.bfloat16
F32 = jnp.float32


def times(left, right):
    return lax.dot_general(left, right, (((1,), (0,)), ((), ())), preferred_element_type=F32)


def times_transposed(left, right):
    return lax.dot_general(left, right, (((1,), (1,)), ((), ())), preferred_element_type=F32)


class Grid:
    def __init__(self, mesh):
        self.count = mesh.shape["fsdp"]
        column = list(mesh.devices[:, 0])
        spots = [tuple(d.coords) for d in column]
        self.cores = 2 if self.count > 1 and spots[0] == spots[1] else 1
        run = 1
        while run < self.count and spots[run][2] == spots[0][2]:
            run += 1
        self.slow = self.count // run
        self.mid = run // self.cores

    def place(self, slow, mid, core):
        return ((slow % self.slow) * self.mid + mid % self.mid) * self.cores + core % self.cores

    def moves(self, slow=0, mid=0, core=0):
        return [
            (self.place(s, m, c), self.place(s + slow, m + mid, c + core))
            for s in range(self.slow)
            for m in range(self.mid)
            for c in range(self.cores)
        ]

    def shift(self, rows, **by):
        return lax.ppermute(rows, "fsdp", self.moves(**by))

    def across(self, slow, step):
        return slow ^ step if self.slow == 4 else (slow + step) % self.slow

    def cross(self, rows, step, ends=True, inner=True):
        moves = []
        for s in range(self.slow):
            if ends if s in (0, self.slow - 1) else inner:
                moves += [
                    (self.place(s, m, c), self.place(self.across(s, step), m, c))
                    for m in range(self.mid)
                    for c in range(self.cores)
                ]
        return lax.ppermute(rows, "fsdp", moves)

    def order(self):
        here = lax.axis_index("fsdp")
        core = here % self.cores
        mid = (here // self.cores) % self.mid
        slow = here // (self.cores * self.mid)
        step = jnp.arange(self.count, dtype=jnp.int32)
        core = (core + step // (self.mid * self.slow)) % self.cores
        mid = (mid + (step // self.slow) % self.mid) % self.mid
        slow = self.across(slow, step % self.slow)
        return ((slow * self.mid + mid) * self.cores + core).astype(jnp.int32)


def flip_kernel(order_ref, rows_ref, out_ref):
    count = order_ref.shape[0]
    block = rows_ref.shape[1] // count

    def move(j, carry):
        start = pl.multiple_of(order_ref[j] * block, block)
        out_ref[pl.ds(pl.multiple_of(j * block, block), block), :] = rows_ref[:, pl.ds(start, block)].T
        return carry

    lax.fori_loop(0, count, move, 0)


def turned(rows, order):
    tokens, width = rows.shape
    count = order.shape[0]
    block = width // count
    if block % 128:
        return rows.T.reshape(count, block, tokens)[order].reshape(width, tokens)
    return pl.pallas_call(
        flip_kernel,
        grid_spec=pltpu.PrefetchScalarGridSpec(
            num_scalar_prefetch=1,
            grid=(1,),
            in_specs=[pl.BlockSpec((tokens, width), lambda i, order: (0, 0))],
            out_specs=pl.BlockSpec((width, tokens), lambda i, order: (0, 0)),
        ),
        out_shape=jax.ShapeDtypeStruct((width, tokens), rows.dtype),
    )(order, rows)


def scatter_product(grid, left, right, relay=False):
    block = left.shape[0] // grid.count
    per_mid = block * grid.slow
    per_core = per_mid * grid.mid
    from_core = []
    for c in range(1, grid.cores):
        out = times(left[c * per_core : (c + 1) * per_core], right).astype(BF16)
        from_core.append(grid.shift(out, core=c))
    from_mid = []
    for m in range(1, grid.mid):
        part = times(left[m * per_mid : (m + 1) * per_mid], right)
        for got in from_core:
            part = part + got[m * per_mid : (m + 1) * per_mid].astype(F32)
        part = part.astype(BF16)
        from_mid.append(grid.shift(part, mid=m))

    def part_of(span):
        part = times(left[span], right)
        for got in from_core + from_mid:
            part = part + got[span].astype(F32)
        return part

    total = part_of(slice(0, block))
    from_slow = []
    if relay and grid.slow == 4:
        mine = part_of(slice(block, 4 * block)).astype(BF16)
        got = grid.cross(mine, 1, inner=False)
        near, far, over = (slice(i * block, (i + 1) * block) for i in range(3))
        from_slow.append(got[near])
        sums = {
            1: mine[near],
            2: (mine[far].astype(F32) + got[over].astype(F32)).astype(BF16),
            3: (mine[over].astype(F32) + got[far].astype(F32)).astype(BF16),
        }
        from_slow += [grid.cross(rows, s, ends=False) for s, rows in sums.items()]
    else:
        for s in range(1, grid.slow):
            part = part_of(slice(s * block, (s + 1) * block)).astype(BF16)
            from_slow.append(grid.cross(part, s))
    for got in from_slow:
        total = total + got.astype(F32)
    return total


def scatter_rows(grid, rows):
    per_core = grid.mid * grid.slow
    total = rows[:per_core]
    for c in range(1, grid.cores):
        total = total + grid.shift(rows[c * per_core : (c + 1) * per_core], core=c)
    rows, total = total, total[: grid.slow]
    for m in range(1, grid.mid):
        total = total + grid.shift(rows[m * grid.slow : (m + 1) * grid.slow], mid=m)
    rows, total = total, total[0]
    for s in range(1, grid.slow):
        total = total + grid.cross(rows[s], s)
    return total


def other(rows):
    return lax.ppermute(rows, "tp", [(0, 1), (1, 0)])


def pair(rows):
    return jnp.concatenate([rows, other(rows)], axis=0)


def collect(term):
    half = term.shape[0] // 2
    return term[:half] + other(term[half:].astype(BF16)).astype(F32)


def norm_forward(rows, gain, shift):
    center = rows - jnp.mean(rows, axis=1, keepdims=True)
    inv_std = lax.rsqrt(jnp.mean(center * center, axis=1, keepdims=True) + EPS)
    normed = center * inv_std
    return (normed * gain + shift, normed, inv_std)


def norm_backward(grad_out, normed, inv_std, gain):
    scaled = grad_out * gain
    grad_in = inv_std * (
        scaled
        - jnp.mean(scaled, axis=1, keepdims=True)
        - normed * jnp.mean(scaled * normed, axis=1, keepdims=True)
    )
    return (grad_in, jnp.sum(grad_out * normed, axis=0), jnp.sum(grad_out, axis=0))


def rope_tables(position):
    half = ROTARY // 2
    inverse = ROPE_BASE ** (-jnp.arange(half).astype(F32) * 2.0 / ROTARY)
    angles = position.astype(F32)[:, None] * inverse[None, :]
    return (jnp.cos(angles)[:, None, :], jnp.sin(angles)[:, None, :])


def rotate(values, cosine, sine):
    half = ROTARY // 2
    first = values[..., :half]
    second = values[..., half:ROTARY]
    return jnp.concatenate(
        [first * cosine - second * sine, second * cosine + first * sine, values[..., ROTARY:]],
        axis=-1,
    )


def masked_scores(queries, key_rows, allowed):
    scores = jnp.einsum("qhd,khd->hqk", queries, key_rows, preferred_element_type=F32) * SCALE
    return jnp.where(allowed, scores, NEG)


def attend(queries, key_rows, value_rows, allowed):
    scores = masked_scores(queries, key_rows, allowed)
    top = jnp.max(scores, axis=-1, keepdims=True)
    log_total = top + jnp.log(jnp.sum(jnp.exp(scores - top), axis=-1, keepdims=True))
    probs = jnp.exp(scores - log_total).astype(BF16)
    mixed = jnp.einsum("hqk,khd->qhd", probs, value_rows, preferred_element_type=F32).astype(BF16)
    return (mixed, log_total)


def attend_back(queries, key_rows, value_rows, mixed, log_total, grad_mixed, allowed):
    scores = masked_scores(queries, key_rows, allowed)
    probs = jnp.exp(scores - log_total)
    grad_values = jnp.einsum("hqk,qhd->khd", probs.astype(BF16), grad_mixed, preferred_element_type=F32)
    grad_probs = jnp.einsum("qhd,khd->hqk", grad_mixed, value_rows, preferred_element_type=F32)
    delta = jnp.sum(grad_mixed.astype(F32) * mixed.astype(F32), axis=-1)
    delta = jnp.transpose(delta, (1, 0))[..., None]
    grad_scores = (probs * (grad_probs - delta) * SCALE).astype(BF16)
    grad_queries = jnp.einsum("hqk,khd->qhd", grad_scores, key_rows, preferred_element_type=F32)
    grad_keys = jnp.einsum("hqk,qhd->khd", grad_scores, queries, preferred_element_type=F32)
    return (grad_queries, grad_keys, grad_values)


def shards(
    grid,
    block_input,
    segments,
    cotangent,
    norm_gain,
    norm_shift,
    qkv_weight,
    qkv_bias,
    out_weight,
    gate_up_weight,
    down_weight,
):
    count = grid.count
    mine = block_input.shape[0]
    length = segments.shape[1]
    width = block_input.shape[1]
    block = width // count
    wide = qkv_weight.shape[3]
    heads = qkv_bias.shape[2]
    piece = qkv_bias.shape[3]
    turn = lax.axis_index("tp")

    small = jnp.concatenate(
        [norm_gain.reshape(-1), norm_shift.reshape(-1), qkv_bias.reshape(-1)]
    )
    n_small = small.shape[0]
    small_rows = 16 * (-(-n_small // (16 * wide)))
    small = jnp.pad(small, (0, small_rows * wide - n_small)).reshape(small_rows, wide)
    pack = jnp.concatenate(
        [qkv_weight[0, :, 0], qkv_weight[0, :, 1], qkv_weight[0, :, 2], out_weight[0].T, small], axis=0
    )
    packs = lax.all_gather(pack, "fsdp", axis=0)
    mlp_pack = jnp.stack([gate_up_weight[0, :, 0], gate_up_weight[0, :, 1], down_weight[0].T])
    mlp_all = lax.all_gather(mlp_pack, "fsdp", axis=1, tiled=True)

    w_q, w_k, w_v, w_out_t = (
        packs[:, i * block : (i + 1) * block].reshape(width, wide) for i in range(4)
    )
    small_all = packs[:, 4 * block :].reshape(count, -1)
    gains = jnp.swapaxes(small_all[:, : 2 * block].reshape(count, 2, block), 0, 1).reshape(2, width)
    shifts = jnp.swapaxes(small_all[:, 2 * block : 4 * block].reshape(count, 2, block), 0, 1).reshape(2, width)
    bias = small_all[:, 4 * block : 4 * block + 3 * heads * piece].reshape(count, 3, heads, piece)
    bias = jnp.transpose(bias, (1, 2, 0, 3)).reshape(3, heads * HEAD).astype(F32)
    gains = gains.astype(F32)
    shifts = shifts.astype(F32)
    w_gate, w_up, w_down_t = mlp_all[0], mlp_all[1], mlp_all[2]

    position = (jnp.arange(length, dtype=jnp.int32) + turn * mine) % length
    cosine, sine = rope_tables(position)
    seg_row = segments[0]
    seg_row = jnp.where(turn == 0, seg_row, jnp.roll(seg_row, mine))
    allowed = (seg_row[:, None] == seg_row[None, :]) & (position[:, None] >= position[None, :])

    order = grid.order()
    down_cot = pair(cotangent)
    down_cot_t = turned(down_cot, order)
    rows_all = pair(block_input).astype(F32)
    resid = block_input.astype(F32)

    first_norm, _, _ = norm_forward(rows_all, gains[0], shifts[0])
    attn_in = first_norm.astype(BF16)
    queries = (times(attn_in, w_q) + bias[0]).reshape(length, heads, HEAD)
    key_rows = (times(attn_in, w_k) + bias[1]).reshape(length, heads, HEAD)
    value_rows = (times(attn_in, w_v) + bias[2]).reshape(length, heads, HEAD)
    queries = rotate(queries, cosine, sine).astype(BF16)
    key_rows = rotate(key_rows, cosine, sine).astype(BF16)
    value_rows = value_rows.astype(BF16)
    mixed, log_total = attend(queries, key_rows, value_rows, allowed)
    mixed_flat = mixed.reshape(length, -1)
    resid_two = resid + collect(times_transposed(mixed_flat, w_out_t))
    second_norm, normed_two, inv_two = norm_forward(resid_two, gains[1], shifts[1])
    mlp_in = pair(second_norm.astype(BF16))
    gate = times(mlp_in, w_gate)
    upper = times(mlp_in, w_up)
    sigma = jax.nn.sigmoid(gate)
    hidden = (gate * sigma * upper).astype(BF16)
    gate, upper, hidden = lax.optimization_barrier((gate, upper, hidden))
    sigma = jax.nn.sigmoid(gate)
    down_grad = scatter_product(grid, down_cot_t, hidden, relay=True)

    grad_three = cotangent.astype(F32)
    grad_hidden = times(down_cot, w_down_t)
    grad_gate = (grad_hidden * upper * sigma * (1.0 + gate * (1.0 - sigma))).astype(BF16)
    grad_up = (grad_hidden * gate * sigma).astype(BF16)
    mlp_in_t = turned(mlp_in, order)
    half = grad_gate.shape[1] // 2
    gate_grad, up_grad = (
        jnp.concatenate(
            [
                scatter_product(grid, mlp_in_t, grad[:, :half], relay=True),
                scatter_product(grid, mlp_in_t, grad[:, half:], relay=True),
            ],
            axis=1,
        )
        for grad in (grad_gate, grad_up)
    )
    grad_mlp_in = collect(times_transposed(grad_gate, w_gate) + times_transposed(grad_up, w_up))
    grad_norm_two, gain_two, shift_two = norm_backward(grad_mlp_in, normed_two, inv_two, gains[1])
    grad_two = grad_three + grad_norm_two
    attn_cot = pair(grad_two.astype(BF16))
    attn_cot, hidden_late = lax.optimization_barrier((attn_cot, hidden))
    resid_three = resid_two + collect(times_transposed(hidden_late, w_down_t))
    block_output = resid_three.astype(BF16)
    grad_mixed = times(attn_cot, w_out_t).astype(BF16).reshape(mixed.shape)
    out_grad = scatter_product(grid, turned(attn_cot, order), mixed_flat)
    grad_queries, grad_keys, grad_values = attend_back(
        queries, key_rows, value_rows, mixed, log_total, grad_mixed, allowed
    )
    grad_queries = rotate(grad_queries, cosine, -sine)
    grad_keys = rotate(grad_keys, cosine, -sine)
    bias_terms = jnp.stack([jnp.sum(g, axis=0) for g in (grad_queries, grad_keys, grad_values)])
    attn_in_t = turned(attn_in, order)
    grad_proj = [g.astype(BF16).reshape(length, -1) for g in (grad_queries, grad_keys, grad_values)]
    v_grad = scatter_product(grid, attn_in_t, grad_proj[2])
    q_grad = scatter_product(grid, attn_in_t, grad_proj[0])
    k_grad = scatter_product(grid, attn_in_t, grad_proj[1])
    grad_attn_in = collect(
        times_transposed(grad_proj[0], w_q)
        + times_transposed(grad_proj[1], w_k)
        + times_transposed(grad_proj[2], w_v),
    )
    _, normed_one, inv_one = norm_forward(resid, gains[0], shifts[0])
    grad_norm_one, gain_one, shift_one = norm_backward(grad_attn_in, normed_one, inv_one, gains[0])
    input_grad = (grad_two + grad_norm_one).astype(BF16)

    gate_up_grad = jnp.stack([gate_grad, up_grad], axis=1)[None]
    norm_terms = jnp.stack([gain_one, gain_two, shift_one, shift_two])
    norm_terms = norm_terms + other(norm_terms)
    norm_terms = jnp.swapaxes(norm_terms.reshape(4, count, block), 0, 1).reshape(count, 4 * block)
    bias_terms = jnp.transpose(bias_terms.reshape(3, heads, count, piece), (2, 0, 1, 3)).reshape(count, -1)
    terms = scatter_rows(grid, jnp.concatenate([norm_terms, bias_terms], axis=1)[order])
    norm_part = terms[: 4 * block].reshape(4, block)
    out_weight_grad = out_grad.T[None]
    qkv_weight_grad = jnp.stack([q_grad, k_grad, v_grad], axis=1)[None]
    bias_part = terms[4 * block :].reshape(3, heads, piece)
    return (
        block_output,
        input_grad,
        norm_part[None, 0:2],
        norm_part[None, 2:4],
        qkv_weight_grad,
        bias_part[None],
        out_weight_grad,
        gate_up_grad,
        down_grad.T[None],
    )


def solution(mesh):
    placed = (
        P(("fsdp", "tp"), None),
        P("fsdp", None),
        P(("fsdp", "tp"), None),
        P(None, None, "fsdp"),
        P(None, None, "fsdp"),
        P(None, "fsdp", None, "tp"),
        P(None, None, "tp", "fsdp"),
        P(None, "tp", "fsdp"),
        P(None, "fsdp", None, "tp"),
        P(None, "tp", "fsdp"),
    )

    def body(*args):
        return shards(Grid(mesh), *args)

    return jax.shard_map(
        body,
        mesh=mesh,
        in_specs=placed,
        out_specs=(
            P(("fsdp", "tp"), None),
            P(("fsdp", "tp"), None),
            P(None, None, "fsdp"),
            P(None, None, "fsdp"),
            P(None, "fsdp", None, "tp"),
            P(None, None, "tp", "fsdp"),
            P(None, "tp", "fsdp"),
            P(None, "fsdp", None, "tp"),
            P(None, "tp", "fsdp"),
        ),
        check_vma=False,
    )
```

```python
import jax
import jax.numpy as jnp
from jax import lax
from jax.experimental import pallas as pl
from jax.experimental.pallas import tpu as pltpu
from jax.sharding import PartitionSpec as P


HEAD = 64
ROTARY = 16

EPS = 1e-05
NEG = -1e30
SCALE = 0.125
ROPE_BASE = 10000.0

BF16 = jnp.bfloat16
F32 = jnp.float32


def times(left, right):
    return lax.dot_general(left, right, (((1,), (0,)), ((), ())), preferred_element_type=F32)


def times_transposed(left, right):
    return lax.dot_general(left, right, (((1,), (1,)), ((), ())), preferred_element_type=F32)


class Grid:
    def __init__(self, mesh):
        self.count = mesh.shape["fsdp"]
        column = list(mesh.devices[:, 0])
        spots = [tuple(d.coords) for d in column]
        self.cores = 2 if self.count > 1 and spots[0] == spots[1] else 1
        run = 1
        while run < self.count and spots[run][2] == spots[0][2]:
            run += 1
        self.slow = self.count // run
        self.mid = run // self.cores

    def place(self, slow, mid, core):
        return ((slow % self.slow) * self.mid + mid % self.mid) * self.cores + core % self.cores

    def moves(self, slow=0, mid=0, core=0):
        return [
            (self.place(s, m, c), self.place(s + slow, m + mid, c + core))
            for s in range(self.slow)
            for m in range(self.mid)
            for c in range(self.cores)
        ]

    def shift(self, rows, **by):
        return lax.ppermute(rows, "fsdp", self.moves(**by))

    def across(self, slow, step):
        return slow ^ step if self.slow == 4 else (slow + step) % self.slow

    def cross(self, rows, step, ends=True, inner=True):
        moves = []
        for s in range(self.slow):
            if ends if s in (0, self.slow - 1) else inner:
                moves += [
                    (self.place(s, m, c), self.place(self.across(s, step), m, c))
                    for m in range(self.mid)
                    for c in range(self.cores)
                ]
        return lax.ppermute(rows, "fsdp", moves)

    def order(self):
        here = lax.axis_index("fsdp")
        core = here % self.cores
        mid = (here // self.cores) % self.mid
        slow = here // (self.cores * self.mid)
        step = jnp.arange(self.count, dtype=jnp.int32)
        core = (core + step // (self.mid * self.slow)) % self.cores
        mid = (mid + (step // self.slow) % self.mid) % self.mid
        slow = self.across(slow, step % self.slow)
        return ((slow * self.mid + mid) * self.cores + core).astype(jnp.int32)


def flip_kernel(order_ref, rows_ref, out_ref):
    count = order_ref.shape[0]
    block = rows_ref.shape[1] // count

    def move(j, carry):
        start = pl.multiple_of(order_ref[j] * block, block)
        out_ref[pl.ds(pl.multiple_of(j * block, block), block), :] = rows_ref[:, pl.ds(start, block)].T
        return carry

    lax.fori_loop(0, count, move, 0)


def turned(rows, order):
    tokens, width = rows.shape
    count = order.shape[0]
    block = width // count
    if block % 128:
        return rows.T.reshape(count, block, tokens)[order].reshape(width, tokens)
    return pl.pallas_call(
        flip_kernel,
        grid_spec=pltpu.PrefetchScalarGridSpec(
            num_scalar_prefetch=1,
            grid=(1,),
            in_specs=[pl.BlockSpec((tokens, width), lambda i, order: (0, 0))],
            out_specs=pl.BlockSpec((width, tokens), lambda i, order: (0, 0)),
        ),
        out_shape=jax.ShapeDtypeStruct((width, tokens), rows.dtype),
    )(order, rows)


def slow_stage(grid, part_of, base, block, relay):
    span = lambda first, last: slice(base + first * block, base + last * block)
    total = part_of(span(0, 1))
    from_slow = []
    if relay and grid.slow == 4:
        mine = part_of(span(1, 4)).astype(BF16)
        got = grid.cross(mine, 1, inner=False)
        near, far, over = (slice(i * block, (i + 1) * block) for i in range(3))
        from_slow.append(got[near])
        sums = {
            1: mine[near],
            2: (mine[far].astype(F32) + got[over].astype(F32)).astype(BF16),
            3: (mine[over].astype(F32) + got[far].astype(F32)).astype(BF16),
        }
        from_slow += [grid.cross(rows, s, ends=False) for s, rows in sums.items()]
    else:
        for s in range(1, grid.slow):
            part = part_of(span(s, s + 1)).astype(BF16)
            from_slow.append(grid.cross(part, s))
    for got in from_slow:
        total = total + got.astype(F32)
    return total


def scatter_product(grid, left, right, relay=False, slow_first=False):
    block = left.shape[0] // grid.count
    per_mid = block * grid.slow
    per_core = per_mid * grid.mid
    from_core = []
    for c in range(1, grid.cores):
        out = times(left[c * per_core : (c + 1) * per_core], right).astype(BF16)
        from_core.append(grid.shift(out, core=c))

    def part_of(span, also=()):
        part = times(left[span], right)
        for got in (*from_core, *also):
            part = part + got[span].astype(F32)
        return part

    if slow_first:
        totals = {
            m: slow_stage(grid, part_of, m * per_mid, block, relay)
            for m in reversed(range(grid.mid))
        }
        total = totals[0]
        for m in range(1, grid.mid):
            part = totals[m].astype(BF16)
            got = grid.shift(part, mid=m)
            total = total + got.astype(F32)
        return total
    from_mid = []
    for m in range(1, grid.mid):
        part = part_of(slice(m * per_mid, (m + 1) * per_mid)).astype(BF16)
        from_mid.append(grid.shift(part, mid=m))
    return slow_stage(grid, lambda span: part_of(span, from_mid), 0, block, relay)


def scatter_rows(grid, rows):
    per_core = grid.mid * grid.slow
    total = rows[:per_core]
    for c in range(1, grid.cores):
        total = total + grid.shift(rows[c * per_core : (c + 1) * per_core], core=c)
    rows, total = total, total[: grid.slow]
    for m in range(1, grid.mid):
        total = total + grid.shift(rows[m * grid.slow : (m + 1) * grid.slow], mid=m)
    rows, total = total, total[0]
    for s in range(1, grid.slow):
        total = total + grid.cross(rows[s], s)
    return total


def other(rows):
    return lax.ppermute(rows, "tp", [(0, 1), (1, 0)])


def pair(rows):
    return jnp.concatenate([rows, other(rows)], axis=0)


def collect(term):
    half = term.shape[0] // 2
    return term[:half] + other(term[half:].astype(BF16)).astype(F32)


def norm_forward(rows, gain, shift):
    center = rows - jnp.mean(rows, axis=1, keepdims=True)
    inv_std = lax.rsqrt(jnp.mean(center * center, axis=1, keepdims=True) + EPS)
    normed = center * inv_std
    return (normed * gain + shift, normed, inv_std)


def norm_backward(grad_out, normed, inv_std, gain):
    scaled = grad_out * gain
    grad_in = inv_std * (
        scaled
        - jnp.mean(scaled, axis=1, keepdims=True)
        - normed * jnp.mean(scaled * normed, axis=1, keepdims=True)
    )
    return (grad_in, jnp.sum(grad_out * normed, axis=0), jnp.sum(grad_out, axis=0))


def rope_tables(position):
    half = ROTARY // 2
    inverse = ROPE_BASE ** (-jnp.arange(half).astype(F32) * 2.0 / ROTARY)
    angles = position.astype(F32)[:, None] * inverse[None, :]
    return (jnp.cos(angles)[:, None, :], jnp.sin(angles)[:, None, :])


def rotate(values, cosine, sine):
    half = ROTARY // 2
    first = values[..., :half]
    second = values[..., half:ROTARY]
    return jnp.concatenate(
        [first * cosine - second * sine, second * cosine + first * sine, values[..., ROTARY:]],
        axis=-1,
    )


def masked_scores(queries, key_rows, allowed):
    scores = jnp.einsum("qhd,khd->hqk", queries, key_rows, preferred_element_type=F32) * SCALE
    return jnp.where(allowed, scores, NEG)


def attend(queries, key_rows, value_rows, allowed):
    scores = masked_scores(queries, key_rows, allowed)
    top = jnp.max(scores, axis=-1, keepdims=True)
    log_total = top + jnp.log(jnp.sum(jnp.exp(scores - top), axis=-1, keepdims=True))
    probs = jnp.exp(scores - log_total).astype(BF16)
    mixed = jnp.einsum("hqk,khd->qhd", probs, value_rows, preferred_element_type=F32).astype(BF16)
    return (mixed, log_total)


def attend_back(queries, key_rows, value_rows, mixed, log_total, grad_mixed, allowed):
    scores = masked_scores(queries, key_rows, allowed)
    probs = jnp.exp(scores - log_total)
    grad_values = jnp.einsum("hqk,qhd->khd", probs.astype(BF16), grad_mixed, preferred_element_type=F32)
    grad_probs = jnp.einsum("qhd,khd->hqk", grad_mixed, value_rows, preferred_element_type=F32)
    delta = jnp.sum(grad_mixed.astype(F32) * mixed.astype(F32), axis=-1)
    delta = jnp.transpose(delta, (1, 0))[..., None]
    grad_scores = (probs * (grad_probs - delta) * SCALE).astype(BF16)
    grad_queries = jnp.einsum("hqk,khd->qhd", grad_scores, key_rows, preferred_element_type=F32)
    grad_keys = jnp.einsum("hqk,qhd->khd", grad_scores, queries, preferred_element_type=F32)
    return (grad_queries, grad_keys, grad_values)


def shards(
    grid,
    block_input,
    segments,
    cotangent,
    norm_gain,
    norm_shift,
    qkv_weight,
    qkv_bias,
    out_weight,
    gate_up_weight,
    down_weight,
):
    count = grid.count
    mine = block_input.shape[0]
    length = segments.shape[1]
    width = block_input.shape[1]
    block = width // count
    wide = qkv_weight.shape[3]
    heads = qkv_bias.shape[2]
    piece = qkv_bias.shape[3]
    turn = lax.axis_index("tp")

    small = jnp.concatenate(
        [norm_gain.reshape(-1), norm_shift.reshape(-1), qkv_bias.reshape(-1)]
    )
    n_small = small.shape[0]
    small_rows = 16 * (-(-n_small // (16 * wide)))
    small = jnp.pad(small, (0, small_rows * wide - n_small)).reshape(small_rows, wide)
    pack = jnp.concatenate(
        [qkv_weight[0, :, 0], qkv_weight[0, :, 1], qkv_weight[0, :, 2], out_weight[0].T, small], axis=0
    )
    packs = lax.all_gather(pack, "fsdp", axis=0)
    mlp_pack = jnp.stack([gate_up_weight[0, :, 0], gate_up_weight[0, :, 1], down_weight[0].T])
    mlp_all = lax.all_gather(mlp_pack, "fsdp", axis=1, tiled=True)

    w_q, w_k, w_v, w_out_t = (
        packs[:, i * block : (i + 1) * block].reshape(width, wide) for i in range(4)
    )
    small_all = packs[:, 4 * block :].reshape(count, -1)
    gains = jnp.swapaxes(small_all[:, : 2 * block].reshape(count, 2, block), 0, 1).reshape(2, width)
    shifts = jnp.swapaxes(small_all[:, 2 * block : 4 * block].reshape(count, 2, block), 0, 1).reshape(2, width)
    bias = small_all[:, 4 * block : 4 * block + 3 * heads * piece].reshape(count, 3, heads, piece)
    bias = jnp.transpose(bias, (1, 2, 0, 3)).reshape(3, heads * HEAD).astype(F32)
    gains = gains.astype(F32)
    shifts = shifts.astype(F32)
    w_gate, w_up, w_down_t = mlp_all[0], mlp_all[1], mlp_all[2]

    position = (jnp.arange(length, dtype=jnp.int32) + turn * mine) % length
    cosine, sine = rope_tables(position)
    seg_row = segments[0]
    seg_row = jnp.where(turn == 0, seg_row, jnp.roll(seg_row, mine))
    allowed = (seg_row[:, None] == seg_row[None, :]) & (position[:, None] >= position[None, :])

    order = grid.order()
    down_cot = pair(cotangent)
    down_cot_t = turned(down_cot, order)
    rows_all = pair(block_input).astype(F32)
    resid = block_input.astype(F32)

    first_norm, _, _ = norm_forward(rows_all, gains[0], shifts[0])
    attn_in = first_norm.astype(BF16)
    queries = (times(attn_in, w_q) + bias[0]).reshape(length, heads, HEAD)
    key_rows = (times(attn_in, w_k) + bias[1]).reshape(length, heads, HEAD)
    value_rows = (times(attn_in, w_v) + bias[2]).reshape(length, heads, HEAD)
    queries = rotate(queries, cosine, sine).astype(BF16)
    key_rows = rotate(key_rows, cosine, sine).astype(BF16)
    value_rows = value_rows.astype(BF16)
    mixed, log_total = attend(queries, key_rows, value_rows, allowed)
    mixed_flat = mixed.reshape(length, -1)
    resid_two = resid + collect(times_transposed(mixed_flat, w_out_t))
    second_norm, normed_two, inv_two = norm_forward(resid_two, gains[1], shifts[1])
    mlp_in = pair(second_norm.astype(BF16))
    gate = times(mlp_in, w_gate)
    upper = times(mlp_in, w_up)
    sigma = jax.nn.sigmoid(gate)
    hidden = (gate * sigma * upper).astype(BF16)
    gate, upper, hidden = lax.optimization_barrier((gate, upper, hidden))
    sigma = jax.nn.sigmoid(gate)
    down_grad = scatter_product(grid, down_cot_t, hidden, relay=True, slow_first=True)

    grad_three = cotangent.astype(F32)
    grad_hidden = times(down_cot, w_down_t)
    grad_gate = (grad_hidden * upper * sigma * (1.0 + gate * (1.0 - sigma))).astype(BF16)
    grad_up = (grad_hidden * gate * sigma).astype(BF16)
    mlp_in_t = turned(mlp_in, order)
    half = grad_gate.shape[1] // 2
    gate_grad, up_grad = (
        jnp.concatenate(
            [
                scatter_product(grid, mlp_in_t, grad[:, :half], relay=True),
                scatter_product(grid, mlp_in_t, grad[:, half:], relay=True),
            ],
            axis=1,
        )
        for grad in (grad_gate, grad_up)
    )
    grad_mlp_in = collect(times_transposed(grad_gate, w_gate) + times_transposed(grad_up, w_up))
    grad_norm_two, gain_two, shift_two = norm_backward(grad_mlp_in, normed_two, inv_two, gains[1])
    grad_two = grad_three + grad_norm_two
    attn_cot = pair(grad_two.astype(BF16))
    attn_cot, hidden_late = lax.optimization_barrier((attn_cot, hidden))
    resid_three = resid_two + collect(times_transposed(hidden_late, w_down_t))
    block_output = resid_three.astype(BF16)
    grad_mixed = times(attn_cot, w_out_t).astype(BF16).reshape(mixed.shape)
    out_grad = scatter_product(grid, turned(attn_cot, order), mixed_flat)
    grad_queries, grad_keys, grad_values = attend_back(
        queries, key_rows, value_rows, mixed, log_total, grad_mixed, allowed
    )
    grad_queries = rotate(grad_queries, cosine, -sine)
    grad_keys = rotate(grad_keys, cosine, -sine)
    bias_terms = jnp.stack([jnp.sum(g, axis=0) for g in (grad_queries, grad_keys, grad_values)])
    attn_in_t = turned(attn_in, order)
    grad_proj = [g.astype(BF16).reshape(length, -1) for g in (grad_queries, grad_keys, grad_values)]
    v_grad = scatter_product(grid, attn_in_t, grad_proj[2])
    q_grad = scatter_product(grid, attn_in_t, grad_proj[0])
    k_grad = scatter_product(grid, attn_in_t, grad_proj[1])
    grad_attn_in = collect(
        times_transposed(grad_proj[0], w_q)
        + times_transposed(grad_proj[1], w_k)
        + times_transposed(grad_proj[2], w_v),
    )
    _, normed_one, inv_one = norm_forward(resid, gains[0], shifts[0])
    grad_norm_one, gain_one, shift_one = norm_backward(grad_attn_in, normed_one, inv_one, gains[0])
    input_grad = (grad_two + grad_norm_one).astype(BF16)

    gate_up_grad = jnp.stack([gate_grad, up_grad], axis=1)[None]
    norm_terms = jnp.stack([gain_one, gain_two, shift_one, shift_two])
    norm_terms = norm_terms + other(norm_terms)
    norm_terms = jnp.swapaxes(norm_terms.reshape(4, count, block), 0, 1).reshape(count, 4 * block)
    bias_terms = jnp.transpose(bias_terms.reshape(3, heads, count, piece), (2, 0, 1, 3)).reshape(count, -1)
    terms = scatter_rows(grid, jnp.concatenate([norm_terms, bias_terms], axis=1)[order])
    norm_part = terms[: 4 * block].reshape(4, block)
    out_weight_grad = out_grad.T[None]
    qkv_weight_grad = jnp.stack([q_grad, k_grad, v_grad], axis=1)[None]
    bias_part = terms[4 * block :].reshape(3, heads, piece)
    return (
        block_output,
        input_grad,
        norm_part[None, 0:2],
        norm_part[None, 2:4],
        qkv_weight_grad,
        bias_part[None],
        out_weight_grad,
        gate_up_grad,
        down_grad.T[None],
    )


def solution(mesh):
    placed = (
        P(("fsdp", "tp"), None),
        P("fsdp", None),
        P(("fsdp", "tp"), None),
        P(None, None, "fsdp"),
        P(None, None, "fsdp"),
        P(None, "fsdp", None, "tp"),
        P(None, None, "tp", "fsdp"),
        P(None, "tp", "fsdp"),
        P(None, "fsdp", None, "tp"),
        P(None, "tp", "fsdp"),
    )

    def body(*args):
        return shards(Grid(mesh), *args)

    return jax.shard_map(
        body,
        mesh=mesh,
        in_specs=placed,
        out_specs=(
            P(("fsdp", "tp"), None),
            P(("fsdp", "tp"), None),
            P(None, None, "fsdp"),
            P(None, None, "fsdp"),
            P(None, "fsdp", None, "tp"),
            P(None, None, "tp", "fsdp"),
            P(None, "tp", "fsdp"),
            P(None, "fsdp", None, "tp"),
            P(None, "tp", "fsdp"),
        ),
        check_vma=False,
    )
```
